32 devices in a mesh: rows: 8 (over z, x), cols: 4 (over y, core).
Axes of the slice: x: 2, y: 2, z: 4, core: 2. Of those that a mesh axis runs over, the one named last changes fastest.
Arguments:
- source_coords: float32 [3, 128, 128], P(None, ('rows', 'cols')), may hold values from -2 to 5
- target_coords: float32 [3, 128, 128], P(None, ('rows', 'cols')), may hold values from -2 to 5
- source_logmass: float32 [128, 128], P(('rows', 'cols')), may hold values from -4 to 134
- target_logmass: float32 [128, 128], P(('rows', 'cols')), may hold values from -4 to 134
- pair_targets: int32 [128, 8], P(('rows', 'cols')), may hold values from 0 to 127, as said below
- pair_counts: int32 [128], P(('rows', 'cols')), may hold values from 1 to 8
Outputs:
- source_potential: float32 [128, 128], P(('rows', 'cols'))
- target_potential: float32 [128, 128], P(('rows', 'cols'))
The draws below stay inside these ranges and needn't reach their ends.
Inputs may be any that keep to these rules, and one draw needn't show every extreme that they name: `pair_targets`: slot 0 of source cluster s holds s itself. Every other used slot names a target cluster held by a device of the same cols index and another rows index. Over the used slots 1 and later of all source clusters of one device, at most 4 name target clusters of one device, and on every device some device is named exactly 4 times. Unused slots hold cluster numbers that are ignored.
All inputs are finite; a program needn't handle non-finite values.
Results may differ from the reference program's by a relative error of at most 0.0003.
Values sent between devices are 32-bit elements; how exact they have to be, the bound alone decides.
No kernel may reach another device: no remote copies, remote signals or barrier semaphores. Data moves between devices by JAX's collectives and lax.ppermute only.
A program may use at most 64 MiB of HBM per device.

```python
import math
import jax
import jax.numpy as jnp
from jax import lax

CL_DEV = 4
PTS = 128
K = 8
C_ITERS = 4
F_ITERS = 2
NCL = 128
CAP = 4
N_ROWS = 8
N_COLS = 4


def cluster_centres(key):
    return jax.random.uniform(jax.random.fold_in(key, 101), (3, NCL), jnp.float32, 0.0, 1.0)


def draw_source_coords(key, part):
    centres = cluster_centres(key)
    jitter = 0.3 * jax.random.truncated_normal(jax.random.fold_in(key, 1), -4.0, 4.0, (3, NCL, PTS), jnp.float32)
    return centres[:, :, None] + jitter


def draw_target_coords(key, part):
    centres = cluster_centres(key)
    moved = 0.15 * jax.random.truncated_normal(jax.random.fold_in(key, 3), -4.0, 4.0, (3, NCL), jnp.float32)
    jitter = 0.3 * jax.random.truncated_normal(jax.random.fold_in(key, 2), -4.0, 4.0, (3, NCL, PTS), jnp.float32)
    return (centres + moved)[:, :, None] + jitter


def shifted_logmass(key, salt):
    levels = jnp.array([0.0, 30.0, 70.0, 100.0, 130.0], jnp.float32)
    picks = jax.random.randint(jax.random.fold_in(key, salt), (NCL,), 0, 5)
    picks = picks.at[0].set(4)
    shift = jnp.take(levels, picks)
    spread = jax.random.truncated_normal(jax.random.fold_in(key, salt + 1), -4.0, 4.0, (NCL, PTS), jnp.float32)
    return shift[:, None] + spread


def draw_source_logmass(key, part):
    return shifted_logmass(key, 301)


def draw_target_logmass(key, part):
    return shifted_logmass(key, 401)


def pair_tables(key):
    base = jax.random.fold_in(key, 202)
    devices = N_ROWS * N_COLS
    remote = K - 1
    chosen = jax.random.randint(jax.random.fold_in(base, 1), (devices,), 0, CL_DEV)
    perm_keys = jax.random.split(jax.random.fold_in(base, 2), devices)
    offsets = jax.vmap(lambda one_key: jax.random.permutation(one_key, N_ROWS - 1))(perm_keys) + 1
    local_ids = jax.random.randint(jax.random.fold_in(base, 3), (devices, CL_DEV, remote), 0, CL_DEV)
    heavy = jax.random.randint(jax.random.fold_in(base, 4), (devices, 1), 0, 2)
    counts = jax.random.randint(jax.random.fold_in(base, 5), (devices, CL_DEV), 1, K + 1)
    rotated = (jnp.arange(CL_DEV)[None, :] - chosen[:, None]) % CL_DEV
    order = rotated[:, :, None] * remote + jnp.arange(remote)[None, None, :]
    groups = order // CAP
    offset = jnp.take_along_axis(offsets, groups.reshape(devices, -1), axis=1).reshape(devices, CL_DEV, remote)
    device_ids = jnp.arange(devices)
    own_row = device_ids // N_COLS
    own_col = device_ids % N_COLS
    owner_row = (own_row[:, None, None] + offset) % N_ROWS
    owner = owner_row * N_COLS + own_col[:, None, None]
    remote_ids = owner * CL_DEV + local_ids
    self_ids = device_ids[:, None] * CL_DEV + jnp.arange(CL_DEV)[None, :]
    filled = rotated < (CAP + remote - 1) // remote
    counts = jnp.where(filled | (heavy == 1), K, counts)
    listed = jnp.concatenate([self_ids[:, :, None], remote_ids], axis=2).reshape(NCL, K)
    return (listed.astype(jnp.int32), counts.reshape(NCL).astype(jnp.int32))


def draw_pair_targets(key, part):
    return pair_tables(key)[0]


def draw_pair_counts(key, part):
    return pair_tables(key)[1]


def setup_inputs(seed: int = 0) -> dict:
    splits = jax.random.split(jax.random.key(seed), 7)
    return {
        "source_coords": draw_source_coords(jax.random.fold_in(splits[6], 71), 0),
        "target_coords": draw_target_coords(jax.random.fold_in(splits[6], 71), 0),
        "source_logmass": draw_source_logmass(jax.random.fold_in(splits[6], 71), 0),
        "target_logmass": draw_target_logmass(jax.random.fold_in(splits[6], 71), 0),
        "pair_targets": draw_pair_targets(jax.random.fold_in(splits[6], 71), 0),
        "pair_counts": draw_pair_counts(jax.random.fold_in(splits[6], 71), 0),
    }


NEGATIVE = -1.0e30
EPS_C = 0.5
EPS_F = 0.1
RHO = 1.0
TAU_C = RHO / (RHO + EPS_C)
TAU_F = RHO / (RHO + EPS_F)


def log_total(values, over_axes):
    highest = jnp.max(values, axis=over_axes, keepdims=True)
    summed = jnp.sum(jnp.exp(values - highest), axis=over_axes)
    return jnp.squeeze(highest, over_axes) + jnp.log(summed)


def coarse_cost(cent_self, cent_other):
    distance = (cent_self[0][:, None] - cent_other[0][None, :]) ** 2
    distance = distance + (cent_self[1][:, None] - cent_other[1][None, :]) ** 2
    distance = distance + (cent_self[2][:, None] - cent_other[2][None, :]) ** 2
    return distance


def coarse_update(pot_other, mass_other, cent_self, cent_other):
    scores = mass_other[None, :] + (pot_other[None, :] - coarse_cost(cent_self, cent_other)) / EPS_C
    return -TAU_C * EPS_C * log_total(scores, 1)


def pair_cost(src_group, tgt_group):
    distance = (src_group[:, 0, None, :, None] - tgt_group[:, 0, :, None, :]) ** 2
    distance = distance + (src_group[:, 1, None, :, None] - tgt_group[:, 1, :, None, :]) ** 2
    distance = distance + (src_group[:, 2, None, :, None] - tgt_group[:, 2, :, None, :]) ** 2
    return distance


def fine_rows(src_group, tgt_group, tgt_mass, tgt_pot, usable):
    distance = pair_cost(src_group, tgt_group)
    scores = tgt_mass[:, :, None, :] + (tgt_pot[:, :, None, :] - distance) / EPS_F
    scores = jnp.where(usable[:, :, None, None], scores, NEGATIVE)
    return -TAU_F * EPS_F * log_total(scores, (1, 3))


def fine_parts(src_group, src_mass, src_pot, tgt_group, usable):
    distance = pair_cost(src_group, tgt_group)
    scores = src_mass[:, None, :, None] + (src_pot[:, None, :, None] - distance) / EPS_F
    highest = jnp.max(scores, axis=2)
    summed = jnp.sum(jnp.exp(scores - highest[:, :, None, :]), axis=2)
    highest = jnp.where(usable[:, :, None], highest, NEGATIVE)
    summed = jnp.where(usable[:, :, None], summed, 0.0)
    return highest, summed


def reference(source_coords, target_coords, source_logmass, target_logmass, pair_targets, pair_counts):
    src_cent = jnp.mean(source_coords, axis=2)
    tgt_cent = jnp.mean(target_coords, axis=2)
    src_mass = log_total(source_logmass, 1)
    tgt_mass = log_total(target_logmass, 1)
    coarse_group = math.gcd(NCL, 512)

    def coarse_all(pot_other, mass_other, cent_self, cent_other):
        portions = cent_self.reshape(3, NCL // coarse_group, coarse_group).transpose(1, 0, 2)
        result = lax.map(lambda portion: coarse_update(pot_other, mass_other, portion, cent_other), portions)
        return result.reshape(NCL)

    tgt_coarse = jnp.zeros((NCL,), jnp.float32)
    for sweep in range(C_ITERS):
        src_coarse = coarse_all(tgt_coarse, tgt_mass, src_cent, tgt_cent)
        tgt_coarse = coarse_all(src_coarse, src_mass, tgt_cent, src_cent)

    tgt_now = jnp.broadcast_to(tgt_coarse[:, None], (NCL, PTS))
    usable = jnp.arange(K)[None, :] < pair_counts[:, None]
    fine_group = math.gcd(NCL, 32)
    src_sorted = source_coords.transpose(1, 0, 2)

    def in_groups(array):
        return array.reshape((NCL // fine_group, fine_group) + array.shape[1:])

    flat_targets = pair_targets.reshape(-1)
    src_now = jnp.zeros((NCL, PTS), jnp.float32)
    for sweep in range(F_ITERS):
        def rows_of(inputs):
            listed, src_group, usable_now = inputs
            tgt_group = target_coords[:, listed].transpose(1, 0, 2, 3)
            return fine_rows(src_group, tgt_group, target_logmass[listed], tgt_now[listed], usable_now)

        src_now = lax.map(rows_of, (in_groups(pair_targets), in_groups(src_sorted), in_groups(usable))).reshape(NCL, PTS)

        def parts_of(inputs):
            listed, src_group, mass_group, pot_group, usable_now = inputs
            tgt_group = target_coords[:, listed].transpose(1, 0, 2, 3)
            return fine_parts(src_group, mass_group, pot_group, tgt_group, usable_now)

        highs, sums = lax.map(parts_of, (in_groups(pair_targets), in_groups(src_sorted), in_groups(source_logmass), in_groups(src_now), in_groups(usable)))
        highs = highs.reshape(NCL * K, PTS)
        sums = sums.reshape(NCL * K, PTS)
        best = jax.ops.segment_max(highs, flat_targets, num_segments=NCL)
        combined = jax.ops.segment_sum(sums * jnp.exp(highs - best[flat_targets]), flat_targets, num_segments=NCL)
        tgt_now = -TAU_F * EPS_F * (best + jnp.log(combined))
    return src_now, tgt_now
```

```python
import math

import jax
import jax.numpy as jnp
from jax import lax
from jax.experimental import pallas as pl
from jax.experimental.pallas import tpu as pltpu
from jax.sharding import PartitionSpec as P

C_ITERS = 4
F_ITERS = 2


NEGATIVE = -1e30
EPS_C = 0.5
EPS_F = 0.1
RHO = 1.0
TAU_C = RHO / (RHO + EPS_C)
TAU_F = RHO / (RHO + EPS_F)


def joined(part, axis, combine):
    gathered = jax.tree.map(lambda a: lax.all_gather(a, axis), part)

    def take(source):
        return jax.tree.map(lambda a: lax.dynamic_index_in_dim(a, source, 0, False), gathered)

    return lax.fori_loop(
        1, lax.axis_size(axis), lambda source, state: combine(state, take(source)), take(0)
    )


def log_total(values, over_axes):
    highest = jnp.max(values, axis=over_axes, keepdims=True)
    summed = jnp.sum(jnp.exp(values - highest), axis=over_axes)
    return jnp.squeeze(highest, over_axes) + jnp.log(summed)


def coarse_cost(cent_self, cent_other):
    distance = (cent_self[0][:, None] - cent_other[0][None, :]) ** 2
    distance = distance + (cent_self[1][:, None] - cent_other[1][None, :]) ** 2
    distance = distance + (cent_self[2][:, None] - cent_other[2][None, :]) ** 2
    return distance


def coarse_update(pot_other, mass_other, cent_self, cent_other):
    scores = mass_other[None, :] + (pot_other[None, :] - coarse_cost(cent_self, cent_other)) / EPS_C
    return -TAU_C * EPS_C * log_total(scores, 1)


def coarse_blocks(pot_other, mass_other, cent_self, cent_other):
    count = cent_self.shape[1]
    width = math.gcd(count, 8)
    portions = cent_self.reshape(3, count // width, width).transpose(1, 0, 2)
    result = lax.map(
        lambda portion: coarse_update(pot_other, mass_other, portion, cent_other), portions
    )
    return result.reshape(count)


def merge_parts(first, second):
    highest = jnp.maximum(first[0], second[0])
    return (
        highest,
        first[1] * jnp.exp(first[0] - highest) + second[1] * jnp.exp(second[0] - highest),
    )


def column_partials(src_mass, src_pot, src_cent, cent_other):
    count = src_cent.shape[1]
    width = math.gcd(count, 8)
    cent_groups = src_cent.reshape(3, count // width, width).transpose(1, 0, 2)
    mass_groups = src_mass.reshape(count // width, width)
    pot_groups = src_pot.reshape(count // width, width)
    columns = cent_other.shape[1]
    start = (jnp.full((columns,), NEGATIVE, jnp.float32), jnp.zeros((columns,), jnp.float32))

    def step(carry, inputs):
        cent_group, mass_group, pot_group = inputs
        scores = (
            mass_group[:, None] + (pot_group[:, None] - coarse_cost(cent_group, cent_other)) / EPS_C
        )
        highest = jnp.max(scores, axis=0)
        summed = jnp.sum(jnp.exp(scores - highest[None, :]), axis=0)
        return (merge_parts(carry, (highest, summed)), None)

    result, unused = lax.scan(step, start, (cent_groups, mass_groups, pot_groups))
    return result


def pair_cost(src_group, tgt_group):
    distance = (src_group[:, 0, None, :, None] - tgt_group[:, 0, :, None, :]) ** 2
    distance = distance + (src_group[:, 1, None, :, None] - tgt_group[:, 1, :, None, :]) ** 2
    distance = distance + (src_group[:, 2, None, :, None] - tgt_group[:, 2, :, None, :]) ** 2
    return distance


def fine_rows(distance, tgt_mass, tgt_pot, usable):
    scores = tgt_mass[:, :, None, :] + (tgt_pot[:, :, None, :] - distance) / EPS_F
    scores = jnp.where(usable[:, :, None, None], scores, NEGATIVE)
    return -TAU_F * EPS_F * log_total(scores, (1, 3))


def fine_parts(distance, src_mass, src_pot, usable):
    scores = src_mass[:, None, :, None] + (src_pot[:, None, :, None] - distance) / EPS_F
    highest = jnp.max(scores, axis=2)
    summed = jnp.sum(jnp.exp(scores - highest[:, :, None, :]), axis=2)
    highest = jnp.where(usable[:, :, None], highest, NEGATIVE)
    summed = jnp.where(usable[:, :, None], summed, 0.0)
    return (highest, summed)


def local_exchanged(source_coords, target_coords, source_logmass, target_logmass, pair_targets, pair_counts):
    clusters = source_coords.shape[1]
    points = source_coords.shape[2]
    listed_slots = pair_targets.shape[1]
    row_count = lax.axis_size("rows")
    col_count = lax.axis_size("cols")
    own_index = lax.axis_index("rows") * col_count + lax.axis_index("cols")
    src_cent = jnp.mean(source_coords, axis=2)
    tgt_cent = jnp.mean(target_coords, axis=2)
    src_mass = log_total(source_logmass, 1)
    tgt_mass = log_total(target_logmass, 1)
    every_tgt = lax.all_gather(
        jnp.concatenate([tgt_cent, tgt_mass[None, :]], 0), ("rows", "cols"), axis=1, tiled=True
    )
    tgt_all = jnp.zeros((every_tgt.shape[1],), jnp.float32)
    for sweep in range(C_ITERS):
        src_own = coarse_blocks(tgt_all, every_tgt[3], src_cent, every_tgt[:3])
        highest, summed = column_partials(src_mass, src_own, src_cent, every_tgt[:3])
        highest, summed = joined((highest, summed), ("rows", "cols"), merge_parts)
        tgt_all = -TAU_C * EPS_C * (highest + jnp.log(summed))
    tgt_own = lax.dynamic_slice_in_dim(tgt_all, own_index * clusters, clusters)
    remote = listed_slots - 1
    capacity = 2 * -(-(clusters * remote) // (2 * (row_count - 1)))
    slot_total = row_count * capacity
    remote_ids = pair_targets[:, 1:]
    owner_row = remote_ids // clusters // col_count
    local_ids = remote_ids % clusters
    remote_used = jnp.arange(1, listed_slots)[None, :] < pair_counts[:, None]
    flat_rows = owner_row.reshape(-1)
    flat_used = remote_used.reshape(-1)
    onehot = ((flat_rows[:, None] == jnp.arange(row_count)[None, :]) & flat_used[:, None]).astype(
        jnp.int32
    )
    before = jnp.cumsum(onehot, axis=0) - onehot
    rank_of = jnp.sum(before * onehot, axis=1)
    slot_of = jnp.where(flat_used, flat_rows * capacity + rank_of, slot_total)
    requests = (
        jnp.full((slot_total,), -1, jnp.int32).at[slot_of].set(local_ids.reshape(-1), mode="drop")
    )
    asked = lax.all_to_all(
        requests.reshape(row_count, capacity), "rows", split_axis=0, concat_axis=0, tiled=True
    )
    asked_flat = asked.reshape(-1)
    asked_index = jnp.maximum(asked_flat, 0)
    own_table = jnp.concatenate([target_coords, target_logmass[None, :, :]], 0)
    sent_cells = own_table[:, asked_index].reshape(4, row_count, capacity, points)
    got_cells = lax.all_to_all(sent_cells, "rows", split_axis=1, concat_axis=1, tiled=True)
    cell_table = jnp.concatenate([own_table, got_cells.reshape(4, slot_total, points)], 1)
    pair_index = jnp.concatenate(
        [
            jnp.arange(clusters)[:, None],
            jnp.where(remote_used, clusters + slot_of.reshape(clusters, remote), 0),
        ],
        1,
    )
    pair_cells = cell_table[:, pair_index].transpose(1, 0, 2, 3)
    usable = jnp.arange(listed_slots)[None, :] < pair_counts[:, None]
    matches = jnp.arange(clusters)[:, None] == asked_flat[None, :]
    match_table = matches.astype(jnp.float32)
    group_size = math.gcd(clusters, 4)
    group_count = clusters // group_size

    def in_groups(array):
        return array.reshape((group_count, group_size) + array.shape[1:])

    src_sorted = source_coords.transpose(1, 0, 2)
    pair_mass = pair_cells[:, 3]
    fcost = lax.map(
        lambda inputs: pair_cost(inputs[0], inputs[1][:, :3]),
        (in_groups(src_sorted), in_groups(pair_cells)),
    )
    tgt_now = jnp.broadcast_to(tgt_own[:, None], (clusters, points))
    src_now = jnp.zeros((clusters, points), jnp.float32)
    for sweep in range(F_ITERS):
        sent_pot = tgt_now[asked_index].reshape(row_count, capacity, points)
        got_pot = lax.all_to_all(sent_pot, "rows", split_axis=0, concat_axis=0, tiled=True)
        pot_table = jnp.concatenate([tgt_now, got_pot.reshape(slot_total, points)], 0)
        pair_pot = pot_table[pair_index]

        def rows_of(inputs):
            cost_group, mass_group, pot_group, usable_now = inputs
            return fine_rows(cost_group, mass_group, pot_group, usable_now)

        src_now = lax.map(
            rows_of, (fcost, in_groups(pair_mass), in_groups(pair_pot), in_groups(usable))
        ).reshape(clusters, points)

        def parts_of(inputs):
            cost_group, mass_group, pot_group, usable_now = inputs
            return fine_parts(cost_group, mass_group, pot_group, usable_now)

        highs, sums = lax.map(
            parts_of, (fcost, in_groups(source_logmass), in_groups(src_now), in_groups(usable))
        )
        highs = highs.reshape(clusters, listed_slots, points)
        sums = sums.reshape(clusters, listed_slots, points)
        back_high = (
            jnp.full((slot_total, points), NEGATIVE, jnp.float32)
            .at[slot_of]
            .set(highs[:, 1:].reshape(-1, points), mode="drop")
        )
        back_sum = (
            jnp.zeros((slot_total, points), jnp.float32)
            .at[slot_of]
            .set(sums[:, 1:].reshape(-1, points), mode="drop")
        )
        got_high, got_sum = (
            lax.all_to_all(
                back_high.reshape(row_count, capacity, points),
                "rows",
                split_axis=0,
                concat_axis=0,
                tiled=True,
            ),
            lax.all_to_all(
                back_sum.reshape(row_count, capacity, points),
                "rows",
                split_axis=0,
                concat_axis=0,
                tiled=True,
            ),
        )
        got_high = got_high.reshape(slot_total, points)
        got_sum = got_sum.reshape(slot_total, points)
        best = jnp.maximum(
            highs[:, 0],
            jnp.max(jnp.where(matches[:, :, None], got_high[None, :, :], NEGATIVE), axis=1),
        )
        scaled = got_sum * jnp.exp(got_high - best[asked_index])
        combined = sums[:, 0] * jnp.exp(highs[:, 0] - best) + jnp.dot(
            match_table, scaled, precision=lax.Precision.HIGHEST
        )
        tgt_now = -TAU_F * EPS_F * (best + jnp.log(combined))
    return (src_now, tgt_now)


GATHERED_MOST = 64
GROUPS = 6
DEPTH = 8 * GROUPS
CENTRE = 1.5
PAIRS_STEP = 8


def three_parts(value):
    first = value.astype(jnp.bfloat16).astype(jnp.float32)
    left = value - first
    second = left.astype(jnp.bfloat16).astype(jnp.float32)
    return first, second, left - second


def coarse_column(stats):
    points = stats.shape[1]
    by_src = jnp.transpose(stats)
    cost = (by_src[:, 0:1] - stats[4:5]) ** 2
    cost = cost + (by_src[:, 1:2] - stats[5:6]) ** 2
    cost = (cost + (by_src[:, 2:3] - stats[6:7]) ** 2) / EPS_C
    to_src = stats[7:8] - cost
    to_tgt = by_src[:, 3:4] - cost
    tgt = jnp.zeros((1, points), jnp.float32)
    for sweep in range(C_ITERS):
        scores = to_src + tgt / EPS_C
        highest = jnp.max(scores, axis=1, keepdims=True)
        summed = jnp.sum(jnp.exp(scores - highest), axis=1, keepdims=True)
        src = -TAU_C * EPS_C * (highest + jnp.log(summed))
        scores = to_tgt + src / EPS_C
        highest = jnp.max(scores, axis=0, keepdims=True)
        summed = jnp.sum(jnp.exp(scores - highest), axis=0, keepdims=True)
        tgt = -TAU_C * EPS_C * (highest + jnp.log(summed))
    return jnp.transpose(jnp.broadcast_to(tgt, (points, points)))


def fine_kernel(
    lists, stats_ref, table, src_rows, tgt_rows, owner, src_out, tgt_out,
    src_right, tgt_right, left, bias, highs, sums, src_pot, tgt_pot,
):
    clusters = table.shape[0]
    points = table.shape[2]
    pairs = highs.shape[0]
    slots = pairs // clusters
    own = src_out.shape[0]
    row_id = lax.broadcasted_iota(jnp.int32, (8, points), 0)

    def grouped(coords, order, extra_row, extra):
        parts = three_parts(coords)
        groups = [parts[part] for part in order]
        for at in range(3):
            groups[at] = jnp.where(row_id == extra_row, extra[at], groups[at])
        return jnp.concatenate(groups, 0)

    src_order = (0, 0, 1, 1, 0, 2)
    tgt_order = (0, 1, 0, 1, 2, 0)

    def src_coords(c):
        return jnp.where(row_id < 3, table[c] - CENTRE, 0.0)

    def tgt_coords(c):
        return jnp.where(row_id < 3, (jnp.roll(table[c], -4, 0) - CENTRE) * (2.0 / EPS_F), 0.0)

    def rights(c, carry):
        ones = (1.0, 1.0, 1.0)
        src_right[c] = grouped(src_coords(c), src_order, 4, ones).astype(jnp.bfloat16)
        tgt_right[c] = grouped(tgt_coords(c), tgt_order, 3, ones).astype(jnp.bfloat16)
        return carry

    def lefts(coords_of, order, extra_row):
        def one(c, carry):
            extra = three_parts(bias[pl.ds(c, 1), :])
            wide = grouped(coords_of(c), order, extra_row, extra)
            left[c] = jnp.transpose(wide).astype(jnp.bfloat16)
            return carry

        lax.fori_loop(0, clusters, one, 0, unroll=4)

    def pair_pass(which, by_target):
        count = lists[4 * pairs + which]

        def step(at, carry):
            for lane in range(PAIRS_STEP):
                place = jnp.minimum(at * PAIRS_STEP + lane, count - 1)
                pair = lists[(1 + which) * pairs + place]
                tgt = lists[pair]
                src = pair // slots
                if by_target:
                    scores = jnp.dot(left[src], tgt_right[tgt], preferred_element_type=jnp.float32)
                else:
                    scores = jnp.dot(left[tgt], src_right[src], preferred_element_type=jnp.float32)
                highest = jnp.max(scores, axis=0, keepdims=True)
                highs[pl.ds(pair, 1), :] = highest
                sums[pl.ds(pair, 1), :] = jnp.sum(jnp.exp(scores - highest), axis=0, keepdims=True)
            return carry

        lax.fori_loop(0, (count + PAIRS_STEP - 1) // PAIRS_STEP, step, 0)

    def src_update():
        high = highs[...].reshape(clusters, slots, points)
        best = jnp.max(high, axis=1)
        total = jnp.sum(sums[...].reshape(clusters, slots, points) * jnp.exp(high - best[:, None, :]), axis=1)
        value = -TAU_F * EPS_F * (best + jnp.log(total) - src_rows[1])
        src_pot[...] = value
        bias[...] = src_rows[0] + value / EPS_F - src_rows[1]

    def tgt_merge(t):
        high = jnp.where(owner[...] == t, highs[...], NEGATIVE)
        best = jnp.max(high, axis=0, keepdims=True)
        total = jnp.sum(sums[...] * jnp.exp(high - best), axis=0, keepdims=True)
        return best + jnp.log(total)

    highs[...] = jnp.full((pairs, points), NEGATIVE, jnp.float32)
    sums[...] = jnp.zeros((pairs, points), jnp.float32)
    lax.fori_loop(0, clusters, rights, 0, unroll=4)
    coarse = coarse_column(stats_ref[...])[:clusters]
    bias[...] = tgt_rows[0] + coarse / EPS_F - tgt_rows[1]
    first_own = lists[4 * pairs + 3]
    for sweep in range(F_ITERS):
        last = sweep == F_ITERS - 1
        lefts(tgt_coords, tgt_order, 4)
        pair_pass(1 if last else 0, False)
        src_update()
        lefts(src_coords, src_order, 3)
        pair_pass(2 if last else 0, True)
        if last:
            for c in range(own):
                t = first_own + c
                tgt_out[pl.ds(c, 1), :] = -TAU_F * EPS_F * (tgt_merge(t) - tgt_rows[1, pl.ds(t, 1), :])
                src_out[pl.ds(c, 1), :] = src_pot[pl.ds(t, 1), :]
        else:

            def merge(t, carry):
                tgt_pot[pl.ds(t, 1), :] = tgt_merge(t)
                return carry

            lax.fori_loop(0, clusters, merge, 0)
            value = -TAU_F * EPS_F * (tgt_pot[...] - tgt_rows[1])
            bias[...] = tgt_rows[0] + value / EPS_F - tgt_rows[1]


def compacted(mask):
    length = mask.shape[1]
    at = jnp.arange(length)
    place = jnp.sum(jnp.where(mask[:, :, None] & (at[:, None] <= at[None, :])[None], 1, 0), axis=1) - 1
    hit = mask[:, :, None] & (place[:, :, None] == at[None, None, :])
    return jnp.sum(jnp.where(hit, at[None, :, None], 0), axis=1), jnp.sum(mask.astype(jnp.int32), axis=1)


def local_gathered(source_coords, target_coords, source_logmass, target_logmass, pair_targets, pair_counts):
    own, points = source_coords.shape[1:]
    slots = pair_targets.shape[1]
    row_count = lax.axis_size("rows")
    col_count = lax.axis_size("cols")
    clusters = own * row_count
    pairs = clusters * slots
    row = lax.axis_index("rows")
    used = jnp.arange(slots)[None, :] < pair_counts[:, None]
    place = pair_targets // (own * col_count) * own + pair_targets % own
    listed = jnp.stack([jnp.where(used, place, 0), used.astype(jnp.int32)]).astype(jnp.float32).reshape(-1)
    listed = jnp.pad(listed, (0, 8 * points - listed.shape[0])).reshape(1, 8, points)
    table = jnp.concatenate(
        [source_coords, source_logmass[None], target_coords, target_logmass[None]], 0
    ).transpose(1, 0, 2)
    packed = jnp.concatenate([table, listed], 0)
    packed = jnp.broadcast_to(packed[None], (row_count,) + packed.shape)
    packed = lax.all_to_all(packed, "rows", split_axis=0, concat_axis=0, tiled=True)
    table = packed[:, :own].reshape(clusters, 8, points)
    listed = packed[:, own, :, :].reshape(row_count, 8 * points)[:, : 2 * own * slots]
    listed = listed.reshape(row_count, 2, own * slots).astype(jnp.int32)
    target_of = listed[:, 0].reshape(pairs)
    used = listed[:, 1].reshape(pairs) > 0

    cent = jnp.mean(table, axis=2)
    stats = jnp.stack(
        [cent[:, 0], cent[:, 1], cent[:, 2], log_total(table[:, 3], 1)]
        + [cent[:, 4], cent[:, 5], cent[:, 6], log_total(table[:, 7], 1)]
    )
    every = [stats]
    for away in range(1, col_count):
        every.append(lax.ppermute(stats, "cols", [(c, c ^ away) for c in range(col_count)]))
    every = jnp.concatenate(every, 1)

    mine = used & (target_of // own == row)
    needed = jnp.any(mine.reshape(clusters, slots), axis=1)
    needed = used & jnp.repeat(needed | (jnp.arange(clusters) // own == row), slots)
    order, counts = compacted(jnp.stack([used, needed, mine]))
    lists = jnp.concatenate(
        [target_of, order.reshape(-1), counts, (row * own)[None], jnp.zeros((4,), jnp.int32)]
    ).astype(jnp.int32)
    owner = jnp.broadcast_to(target_of[:, None], (pairs, points))
    centred = table - CENTRE
    src_rows = jnp.stack([table[:, 3], jnp.sum(centred[:, :3] ** 2, axis=1) / EPS_F])
    tgt_rows = jnp.stack([table[:, 7], jnp.sum(centred[:, 4:7] ** 2, axis=1) / EPS_F])
    whole = pl.BlockSpec(memory_space=pltpu.VMEM)
    return pl.pallas_call(
        fine_kernel,
        out_shape=(jax.ShapeDtypeStruct((own, points), jnp.float32),) * 2,
        in_specs=[pl.BlockSpec(memory_space=pltpu.SMEM)] + [whole] * 5,
        out_specs=(whole, whole),
        scratch_shapes=[
            pltpu.VMEM((clusters, DEPTH, points), jnp.bfloat16),
            pltpu.VMEM((clusters, DEPTH, points), jnp.bfloat16),
            pltpu.VMEM((clusters, points, DEPTH), jnp.bfloat16),
            pltpu.VMEM((clusters, points), jnp.float32),
            pltpu.VMEM((pairs, points), jnp.float32),
            pltpu.VMEM((pairs, points), jnp.float32),
            pltpu.VMEM((clusters, points), jnp.float32),
            pltpu.VMEM((clusters, points), jnp.float32),
        ],
        name="fine",
    )(lists, every, table, src_rows, tgt_rows, owner)


def solution(mesh):
    columns = mesh.shape["rows"]

    def local(*args):
        clusters, points = args[0].shape[1:]
        if clusters * columns <= GATHERED_MOST and clusters * columns * mesh.shape["cols"] == points:
            return local_gathered(*args)
        return local_exchanged(*args)

    return jax.shard_map(
        local,
        mesh=mesh,
        in_specs=(
            P(None, ("rows", "cols"), None),
            P(None, ("rows", "cols"), None),
            P(("rows", "cols"), None),
            P(("rows", "cols"), None),
            P(("rows", "cols"), None),
            P(("rows", "cols")),
        ),
        out_specs=(P(("rows", "cols"), None), P(("rows", "cols"), None)),
        check_vma=False,
    )
```

```python
import math

import jax
import jax.numpy as jnp
from jax import lax
from jax.experimental import pallas as pl
from jax.experimental.pallas import tpu as pltpu
from jax.sharding import PartitionSpec as P

C_ITERS = 4
F_ITERS = 2


NEGATIVE = -1e30
EPS_C = 0.5
EPS_F = 0.1
RHO = 1.0
TAU_C = RHO / (RHO + EPS_C)
TAU_F = RHO / (RHO + EPS_F)


def joined(part, axis, combine):
    gathered = jax.tree.map(lambda a: lax.all_gather(a, axis), part)

    def take(source):
        return jax.tree.map(lambda a: lax.dynamic_index_in_dim(a, source, 0, False), gathered)

    return lax.fori_loop(
        1, lax.axis_size(axis), lambda source, state: combine(state, take(source)), take(0)
    )


def log_total(values, over_axes):
    highest = jnp.max(values, axis=over_axes, keepdims=True)
    summed = jnp.sum(jnp.exp(values - highest), axis=over_axes)
    return jnp.squeeze(highest, over_axes) + jnp.log(summed)


def coarse_cost(cent_self, cent_other):
    distance = (cent_self[0][:, None] - cent_other[0][None, :]) ** 2
    distance = distance + (cent_self[1][:, None] - cent_other[1][None, :]) ** 2
    distance = distance + (cent_self[2][:, None] - cent_other[2][None, :]) ** 2
    return distance


def coarse_update(pot_other, mass_other, cent_self, cent_other):
    scores = mass_other[None, :] + (pot_other[None, :] - coarse_cost(cent_self, cent_other)) / EPS_C
    return -TAU_C * EPS_C * log_total(scores, 1)


def coarse_blocks(pot_other, mass_other, cent_self, cent_other):
    count = cent_self.shape[1]
    width = math.gcd(count, 8)
    portions = cent_self.reshape(3, count // width, width).transpose(1, 0, 2)
    result = lax.map(
        lambda portion: coarse_update(pot_other, mass_other, portion, cent_other), portions
    )
    return result.reshape(count)


def merge_parts(first, second):
    highest = jnp.maximum(first[0], second[0])
    return (
        highest,
        first[1] * jnp.exp(first[0] - highest) + second[1] * jnp.exp(second[0] - highest),
    )


def column_partials(src_mass, src_pot, src_cent, cent_other):
    count = src_cent.shape[1]
    width = math.gcd(count, 8)
    cent_groups = src_cent.reshape(3, count // width, width).transpose(1, 0, 2)
    mass_groups = src_mass.reshape(count // width, width)
    pot_groups = src_pot.reshape(count // width, width)
    columns = cent_other.shape[1]
    start = (jnp.full((columns,), NEGATIVE, jnp.float32), jnp.zeros((columns,), jnp.float32))

    def step(carry, inputs):
        cent_group, mass_group, pot_group = inputs
        scores = (
            mass_group[:, None] + (pot_group[:, None] - coarse_cost(cent_group, cent_other)) / EPS_C
        )
        highest = jnp.max(scores, axis=0)
        summed = jnp.sum(jnp.exp(scores - highest[None, :]), axis=0)
        return (merge_parts(carry, (highest, summed)), None)

    result, unused = lax.scan(step, start, (cent_groups, mass_groups, pot_groups))
    return result


def pair_cost(src_group, tgt_group):
    distance = (src_group[:, 0, None, :, None] - tgt_group[:, 0, :, None, :]) ** 2
    distance = distance + (src_group[:, 1, None, :, None] - tgt_group[:, 1, :, None, :]) ** 2
    distance = distance + (src_group[:, 2, None, :, None] - tgt_group[:, 2, :, None, :]) ** 2
    return distance


def fine_rows(distance, tgt_mass, tgt_pot, usable):
    scores = tgt_mass[:, :, None, :] + (tgt_pot[:, :, None, :] - distance) / EPS_F
    scores = jnp.where(usable[:, :, None, None], scores, NEGATIVE)
    return -TAU_F * EPS_F * log_total(scores, (1, 3))


def fine_parts(distance, src_mass, src_pot, usable):
    scores = src_mass[:, None, :, None] + (src_pot[:, None, :, None] - distance) / EPS_F
    highest = jnp.max(scores, axis=2)
    summed = jnp.sum(jnp.exp(scores - highest[:, :, None, :]), axis=2)
    highest = jnp.where(usable[:, :, None], highest, NEGATIVE)
    summed = jnp.where(usable[:, :, None], summed, 0.0)
    return (highest, summed)


def local_exchanged(source_coords, target_coords, source_logmass, target_logmass, pair_targets, pair_counts):
    clusters = source_coords.shape[1]
    points = source_coords.shape[2]
    listed_slots = pair_targets.shape[1]
    row_count = lax.axis_size("rows")
    col_count = lax.axis_size("cols")
    own_index = lax.axis_index("rows") * col_count + lax.axis_index("cols")
    src_cent = jnp.mean(source_coords, axis=2)
    tgt_cent = jnp.mean(target_coords, axis=2)
    src_mass = log_total(source_logmass, 1)
    tgt_mass = log_total(target_logmass, 1)
    every_tgt = lax.all_gather(
        jnp.concatenate([tgt_cent, tgt_mass[None, :]], 0), ("rows", "cols"), axis=1, tiled=True
    )
    tgt_all = jnp.zeros((every_tgt.shape[1],), jnp.float32)
    for sweep in range(C_ITERS):
        src_own = coarse_blocks(tgt_all, every_tgt[3], src_cent, every_tgt[:3])
        highest, summed = column_partials(src_mass, src_own, src_cent, every_tgt[:3])
        highest, summed = joined((highest, summed), ("rows", "cols"), merge_parts)
        tgt_all = -TAU_C * EPS_C * (highest + jnp.log(summed))
    tgt_own = lax.dynamic_slice_in_dim(tgt_all, own_index * clusters, clusters)
    remote = listed_slots - 1
    capacity = 2 * -(-(clusters * remote) // (2 * (row_count - 1)))
    slot_total = row_count * capacity
    remote_ids = pair_targets[:, 1:]
    owner_row = remote_ids // clusters // col_count
    local_ids = remote_ids % clusters
    remote_used = jnp.arange(1, listed_slots)[None, :] < pair_counts[:, None]
    flat_rows = owner_row.reshape(-1)
    flat_used = remote_used.reshape(-1)
    onehot = ((flat_rows[:, None] == jnp.arange(row_count)[None, :]) & flat_used[:, None]).astype(
        jnp.int32
    )
    before = jnp.cumsum(onehot, axis=0) - onehot
    rank_of = jnp.sum(before * onehot, axis=1)
    slot_of = jnp.where(flat_used, flat_rows * capacity + rank_of, slot_total)
    requests = (
        jnp.full((slot_total,), -1, jnp.int32).at[slot_of].set(local_ids.reshape(-1), mode="drop")
    )
    asked = lax.all_to_all(
        requests.reshape(row_count, capacity), "rows", split_axis=0, concat_axis=0, tiled=True
    )
    asked_flat = asked.reshape(-1)
    asked_index = jnp.maximum(asked_flat, 0)
    own_table = jnp.concatenate([target_coords, target_logmass[None, :, :]], 0)
    sent_cells = own_table[:, asked_index].reshape(4, row_count, capacity, points)
    got_cells = lax.all_to_all(sent_cells, "rows", split_axis=1, concat_axis=1, tiled=True)
    cell_table = jnp.concatenate([own_table, got_cells.reshape(4, slot_total, points)], 1)
    pair_index = jnp.concatenate(
        [
            jnp.arange(clusters)[:, None],
            jnp.where(remote_used, clusters + slot_of.reshape(clusters, remote), 0),
        ],
        1,
    )
    pair_cells = cell_table[:, pair_index].transpose(1, 0, 2, 3)
    usable = jnp.arange(listed_slots)[None, :] < pair_counts[:, None]
    matches = jnp.arange(clusters)[:, None] == asked_flat[None, :]
    match_table = matches.astype(jnp.float32)
    group_size = math.gcd(clusters, 4)
    group_count = clusters // group_size

    def in_groups(array):
        return array.reshape((group_count, group_size) + array.shape[1:])

    src_sorted = source_coords.transpose(1, 0, 2)
    pair_mass = pair_cells[:, 3]
    fcost = lax.map(
        lambda inputs: pair_cost(inputs[0], inputs[1][:, :3]),
        (in_groups(src_sorted), in_groups(pair_cells)),
    )
    tgt_now = jnp.broadcast_to(tgt_own[:, None], (clusters, points))
    src_now = jnp.zeros((clusters, points), jnp.float32)
    for sweep in range(F_ITERS):
        sent_pot = tgt_now[asked_index].reshape(row_count, capacity, points)
        got_pot = lax.all_to_all(sent_pot, "rows", split_axis=0, concat_axis=0, tiled=True)
        pot_table = jnp.concatenate([tgt_now, got_pot.reshape(slot_total, points)], 0)
        pair_pot = pot_table[pair_index]

        def rows_of(inputs):
            cost_group, mass_group, pot_group, usable_now = inputs
            return fine_rows(cost_group, mass_group, pot_group, usable_now)

        src_now = lax.map(
            rows_of, (fcost, in_groups(pair_mass), in_groups(pair_pot), in_groups(usable))
        ).reshape(clusters, points)

        def parts_of(inputs):
            cost_group, mass_group, pot_group, usable_now = inputs
            return fine_parts(cost_group, mass_group, pot_group, usable_now)

        highs, sums = lax.map(
            parts_of, (fcost, in_groups(source_logmass), in_groups(src_now), in_groups(usable))
        )
        highs = highs.reshape(clusters, listed_slots, points)
        sums = sums.reshape(clusters, listed_slots, points)
        back_high = (
            jnp.full((slot_total, points), NEGATIVE, jnp.float32)
            .at[slot_of]
            .set(highs[:, 1:].reshape(-1, points), mode="drop")
        )
        back_sum = (
            jnp.zeros((slot_total, points), jnp.float32)
            .at[slot_of]
            .set(sums[:, 1:].reshape(-1, points), mode="drop")
        )
        got_high, got_sum = (
            lax.all_to_all(
                back_high.reshape(row_count, capacity, points),
                "rows",
                split_axis=0,
                concat_axis=0,
                tiled=True,
            ),
            lax.all_to_all(
                back_sum.reshape(row_count, capacity, points),
                "rows",
                split_axis=0,
                concat_axis=0,
                tiled=True,
            ),
        )
        got_high = got_high.reshape(slot_total, points)
        got_sum = got_sum.reshape(slot_total, points)
        best = jnp.maximum(
            highs[:, 0],
            jnp.max(jnp.where(matches[:, :, None], got_high[None, :, :], NEGATIVE), axis=1),
        )
        scaled = got_sum * jnp.exp(got_high - best[asked_index])
        combined = sums[:, 0] * jnp.exp(highs[:, 0] - best) + jnp.dot(
            match_table, scaled, precision=lax.Precision.HIGHEST
        )
        tgt_now = -TAU_F * EPS_F * (best + jnp.log(combined))
    return (src_now, tgt_now)


FEATURES = 32
CENTRE = 1.5
GROUP = 8
LOG2E = math.log2(math.e)
LN2 = math.log(2.0)


def three_parts(value):
    first = value.astype(jnp.bfloat16).astype(jnp.float32)
    left = value - first
    second = left.astype(jnp.bfloat16).astype(jnp.float32)
    return first, second, left - second


def coarse_start(stats):
    by_src = jnp.transpose(stats)
    cost = (by_src[:, 0:1] - stats[4:5]) ** 2
    cost = cost + (by_src[:, 1:2] - stats[5:6]) ** 2
    cost = (cost + (by_src[:, 2:3] - stats[6:7]) ** 2) / EPS_C
    return stats[7:8] - cost, by_src[:, 3:4] - cost


def coarse_sweep(to_src, to_tgt, tgt):
    scores = to_src + tgt / EPS_C
    highest = jnp.max(scores, axis=1, keepdims=True)
    summed = jnp.sum(jnp.exp(scores - highest), axis=1, keepdims=True)
    src = -TAU_C * EPS_C * (highest + jnp.log(summed))
    scores = to_tgt + src / EPS_C
    highest = jnp.max(scores, axis=0, keepdims=True)
    summed = jnp.sum(jnp.exp(scores - highest), axis=0, keepdims=True)
    return -TAU_C * EPS_C * (highest + jnp.log(summed))


def fine_kernel(
    lists, stats_ref, table, src_rows, tgt_rows, owner, owner_row, src_out, tgt_out,
    src_right, tgt_right, src_left, tgt_left, parts_ref, even, odd, highs, sums, src_pot, best_rows, to_src, to_tgt,
):
    clusters = table.shape[0]
    points = table.shape[2]
    pairs = highs.shape[0]
    slots = pairs // clusters
    own = src_out.shape[0]
    counts_at = pairs + 3 * (pairs + 2 * GROUP)
    row_id = lax.broadcasted_iota(jnp.int32, (8, points), 0)

    def features(coords, order):
        parts = three_parts(coords)
        groups = [parts[one] + jnp.roll(parts[two], 3, 0) for one, two in order]
        return jnp.concatenate(groups + [jnp.where(row_id < 3, 1.0, 0.0)], 0)

    def prepare(c):
        coords = jnp.where(row_id < 3, table[c] - CENTRE, 0.0)
        wide = features(coords, ((0, 0), (1, 1), (0, 2)))
        src_right[c] = wide.astype(jnp.bfloat16)
        src_left[c] = jnp.transpose(wide).astype(jnp.bfloat16)
        coords = jnp.where(row_id < 3, (jnp.roll(table[c], -4, 0) - CENTRE) * (2.0 / EPS_F * LOG2E), 0.0)
        wide = features(coords, ((0, 1), (0, 1), (2, 0)))
        tgt_right[c] = wide.astype(jnp.bfloat16)
        tgt_left[c] = jnp.transpose(wide).astype(jnp.bfloat16)

    def spread(bias, left):
        for part, value in enumerate(three_parts(bias * LOG2E)):
            parts_ref[:, part, :] = value
        by_point = jnp.transpose(parts_ref[...].reshape(4 * clusters, points))
        for c in range(clusters):
            shift = (FEATURES - 8 - 4 * c) % (4 * clusters)
            moved = pltpu.roll(by_point, shift, 1) if shift else by_point
            left[c, :, FEATURES - 8 : FEATURES - 4] = moved[:, FEATURES - 8 : FEATURES - 4].astype(jnp.bfloat16)

    def pair_pass(which, by_target):
        left, right = (src_left, tgt_right) if by_target else (tgt_left, src_right)

        first = pairs + which * (pairs + 2 * GROUP)

        def score(group, lane, buffer):
            pair = lists[first + group * GROUP + lane]
            src, tgt = lax.shift_right_logical(pair, slots.bit_length() - 1), lists[pair]
            row, col = (src, tgt) if by_target else (tgt, src)
            buffer[lane] = jnp.dot(left[row], right[col], preferred_element_type=jnp.float32)

        def reduce(group, lane, buffer):
            pair = lists[first + group * GROUP + lane]
            scores = buffer[lane]
            highest = jnp.max(scores, axis=0, keepdims=True)
            highs[pl.ds(pair, 1), :] = highest
            sums[pl.ds(pair, 1), :] = jnp.sum(jnp.exp2(scores - highest), axis=0, keepdims=True)

        def step(at, carry):
            for group, ready, filled in ((2 * at, even, odd), (2 * at + 1, odd, even)):
                for lane in range(GROUP):
                    score(group + 1, lane, filled)
                    reduce(group, lane, ready)
            return carry

        for lane in range(GROUP):
            score(0, lane, even)
        lax.fori_loop(0, lists[counts_at + which], step, 0)

    def src_update():
        high = highs[...].reshape(clusters, slots, points)
        best = jnp.max(high, axis=1)
        total = jnp.sum(sums[...].reshape(clusters, slots, points) * jnp.exp2(high - best[:, None, :]), axis=1)
        value = -TAU_F * EPS_F * (LN2 * (best + jnp.log2(total)) - src_rows[1])
        src_pot[...] = value
        return src_rows[0] + value / EPS_F - src_rows[1]

    def best_of(t):
        return jnp.max(jnp.where(owner[...] == t, highs[...], NEGATIVE), axis=0, keepdims=True)

    def tgt_merge():
        width = math.gcd(clusters, 4)

        def find(at, carry):
            for step in range(width):
                best_rows[pl.ds(at * width + step, 1), :] = best_of(at * width + step)
            return carry

        lax.fori_loop(0, clusters // width, find, 0)
        best = best_rows[...]
        lane = lax.broadcasted_iota(jnp.int32, (pairs, points), 1)
        picks = jnp.where((lane >= FEATURES) & (lane % clusters == owner[...]), 1.0, 0.0).astype(jnp.bfloat16)
        parts = jnp.concatenate((jnp.zeros((FEATURES, points), jnp.float32),) + three_parts(best), 0)
        by_pair = jnp.dot(picks, parts.astype(jnp.bfloat16), preferred_element_type=jnp.float32)
        weighted = three_parts(sums[...] * jnp.exp2(highs[...] - by_pair))
        row = lax.broadcasted_iota(jnp.int32, (clusters, pairs), 0)
        gather = jnp.where(row == owner_row[...], 1.0, 0.0).astype(jnp.bfloat16)
        total = sum(
            jnp.dot(gather, part.astype(jnp.bfloat16), preferred_element_type=jnp.float32) for part in weighted
        )
        return LN2 * (best + jnp.log2(total))

    parts_ref[...] = jnp.zeros((clusters, 4, points), jnp.float32)
    highs[...] = jnp.full((pairs, points), NEGATIVE, jnp.float32)
    sums[...] = jnp.zeros((pairs, points), jnp.float32)
    to_src[...], to_tgt[...] = coarse_start(stats_ref[...])

    def begin(at, tgt):
        for c in range(clusters // C_ITERS):
            prepare(at * (clusters // C_ITERS) + c)
        return coarse_sweep(to_src[...], to_tgt[...], tgt)

    coarse = lax.fori_loop(0, C_ITERS, begin, jnp.zeros((1, points), jnp.float32))
    coarse = jnp.transpose(jnp.broadcast_to(coarse, (points, points)))[:clusters]
    tgt_bias = tgt_rows[0] + coarse / EPS_F - tgt_rows[1]
    first_own = lists[counts_at + 3]
    for sweep in range(F_ITERS):
        last = sweep == F_ITERS - 1
        spread(tgt_bias, tgt_left)
        pair_pass(1 if last else 0, False)
        spread(src_update(), src_left)
        pair_pass(2 if last else 0, True)
        if not last:
            value = -TAU_F * EPS_F * (tgt_merge() - tgt_rows[1])
            tgt_bias = tgt_rows[0] + value / EPS_F - tgt_rows[1]
    for c in range(own):
        t = first_own + c
        best = best_of(t)
        mine = jnp.where(owner[...] == t, sums[...] * jnp.exp2(highs[...] - best), 0.0)
        total = LN2 * (best + jnp.log2(jnp.sum(mine, axis=0, keepdims=True)))
        tgt_out[pl.ds(c, 1), :] = -TAU_F * EPS_F * (total - tgt_rows[1, pl.ds(t, 1), :])
        src_out[pl.ds(c, 1), :] = src_pot[pl.ds(t, 1), :]


def compacted(mask):
    length = mask.shape[1]
    at = jnp.arange(length)
    place = jnp.sum(jnp.where(mask[:, :, None] & (at[:, None] <= at[None, :])[None], 1, 0), axis=1) - 1
    hit = mask[:, :, None] & (place[:, :, None] == at[None, None, :])
    return jnp.sum(jnp.where(hit, at[None, :, None], 0), axis=1), jnp.sum(mask.astype(jnp.int32), axis=1)


def local_gathered(source_coords, target_coords, source_logmass, target_logmass, pair_targets, pair_counts):
    own, points = source_coords.shape[1:]
    slots = pair_targets.shape[1]
    row_count = lax.axis_size("rows")
    col_count = lax.axis_size("cols")
    clusters = own * row_count
    pairs = clusters * slots
    row = lax.axis_index("rows")
    used = jnp.arange(slots)[None, :] < pair_counts[:, None]
    place = pair_targets // (own * col_count) * own + pair_targets % own
    listed = jnp.stack([jnp.where(used, place, 0), used.astype(jnp.int32)]).astype(jnp.float32).reshape(-1)
    listed = jnp.pad(listed, (0, 8 * points - listed.shape[0])).reshape(1, 8, points)
    table = jnp.concatenate(
        [source_coords, source_logmass[None], target_coords, target_logmass[None]], 0
    ).transpose(1, 0, 2)
    packed = jnp.concatenate([table, listed], 0)
    packed = jnp.broadcast_to(packed[None], (row_count,) + packed.shape)
    packed = lax.all_to_all(packed, "rows", split_axis=0, concat_axis=0, tiled=True)
    table = packed[:, :own].reshape(clusters, 8, points)
    listed = packed[:, own, :, :].reshape(row_count, 8 * points)[:, : 2 * own * slots]
    listed = listed.reshape(row_count, 2, own * slots).astype(jnp.int32)
    target_of = listed[:, 0].reshape(pairs)
    used = listed[:, 1].reshape(pairs) > 0

    cent = jnp.mean(table, axis=2)
    stats = jnp.stack(
        [cent[:, 0], cent[:, 1], cent[:, 2], log_total(table[:, 3], 1)]
        + [cent[:, 4], cent[:, 5], cent[:, 6], log_total(table[:, 7], 1)]
    )
    every = [stats]
    for away in range(1, col_count):
        every.append(lax.ppermute(stats, "cols", [(c, c ^ away) for c in range(col_count)]))
    every = jnp.concatenate(every, 1)

    mine = used & (target_of // own == row)
    needed = jnp.any(mine.reshape(clusters, slots), axis=1)
    needed = used & jnp.repeat(needed | (jnp.arange(clusters) // own == row), slots)
    order, counts = compacted(jnp.stack([used, needed, mine]))
    order = jnp.pad(order, ((0, 0), (0, 2 * GROUP)))
    counts = (counts + 2 * GROUP - 1) // (2 * GROUP)
    lists = jnp.concatenate(
        [target_of, order.reshape(-1), counts, (row * own)[None], jnp.zeros((4,), jnp.int32)]
    ).astype(jnp.int32)
    owner = jnp.broadcast_to(target_of[:, None], (pairs, points))
    centred = table - CENTRE
    src_rows = jnp.stack([table[:, 3], jnp.sum(centred[:, :3] ** 2, axis=1) / EPS_F])
    tgt_rows = jnp.stack([table[:, 7], jnp.sum(centred[:, 4:7] ** 2, axis=1) / EPS_F])
    whole = pl.BlockSpec(memory_space=pltpu.VMEM)
    return pl.pallas_call(
        fine_kernel,
        out_shape=(jax.ShapeDtypeStruct((own, points), jnp.float32),) * 2,
        in_specs=[pl.BlockSpec(memory_space=pltpu.SMEM)] + [whole] * 6,
        out_specs=(whole, whole),
        scratch_shapes=[
            pltpu.VMEM((clusters, FEATURES, points), jnp.bfloat16),
            pltpu.VMEM((clusters, FEATURES, points), jnp.bfloat16),
            pltpu.VMEM((clusters, points, FEATURES), jnp.bfloat16),
            pltpu.VMEM((clusters, points, FEATURES), jnp.bfloat16),
            pltpu.VMEM((clusters, 4, points), jnp.float32),
            pltpu.VMEM((GROUP, points, points), jnp.float32),
            pltpu.VMEM((GROUP, points, points), jnp.float32),
            pltpu.VMEM((pairs, points), jnp.float32),
            pltpu.VMEM((pairs, points), jnp.float32),
            pltpu.VMEM((clusters, points), jnp.float32),
            pltpu.VMEM((clusters, points), jnp.float32),
            pltpu.VMEM((points, points), jnp.float32),
            pltpu.VMEM((points, points), jnp.float32),
        ],
        compiler_params=pltpu.CompilerParams(vmem_limit_bytes=12 * 2**20),
        name="fine",
    )(lists, every, table, src_rows, tgt_rows, owner, target_of[None])


def solution(mesh):
    columns = mesh.shape["rows"]

    def local(*args):
        clusters, points = args[0].shape[1:]
        if columns * clusters * mesh.shape["cols"] == points == FEATURES + 3 * clusters * columns:
            return local_gathered(*args)
        return local_exchanged(*args)

    return jax.shard_map(
        local,
        mesh=mesh,
        in_specs=(
            P(None, ("rows", "cols"), None),
            P(None, ("rows", "cols"), None),
            P(("rows", "cols"), None),
            P(("rows", "cols"), None),
            P(("rows", "cols"), None),
            P(("rows", "cols")),
        ),
        out_specs=(P(("rows", "cols"), None), P(("rows", "cols"), None)),
        check_vma=False,
    )
```

```python
import math

import jax
import jax.numpy as jnp
from jax import lax
from jax.experimental import pallas as pl
from jax.experimental.pallas import tpu as pltpu
from jax.sharding import PartitionSpec as P

C_ITERS = 4
F_ITERS = 2


NEGATIVE = -1e30
EPS_C = 0.5
EPS_F = 0.1
RHO = 1.0
TAU_C = RHO / (RHO + EPS_C)
TAU_F = RHO / (RHO + EPS_F)


def joined(part, axis, combine):
    gathered = jax.tree.map(lambda a: lax.all_gather(a, axis), part)

    def take(source):
        return jax.tree.map(lambda a: lax.dynamic_index_in_dim(a, source, 0, False), gathered)

    return lax.fori_loop(
        1, lax.axis_size(axis), lambda source, state: combine(state, take(source)), take(0)
    )


def log_total(values, over_axes):
    highest = jnp.max(values, axis=over_axes, keepdims=True)
    summed = jnp.sum(jnp.exp(values - highest), axis=over_axes)
    return jnp.squeeze(highest, over_axes) + jnp.log(summed)


def coarse_cost(cent_self, cent_other):
    distance = (cent_self[0][:, None] - cent_other[0][None, :]) ** 2
    distance = distance + (cent_self[1][:, None] - cent_other[1][None, :]) ** 2
    distance = distance + (cent_self[2][:, None] - cent_other[2][None, :]) ** 2
    return distance


def coarse_update(pot_other, mass_other, cent_self, cent_other):
    scores = mass_other[None, :] + (pot_other[None, :] - coarse_cost(cent_self, cent_other)) / EPS_C
    return -TAU_C * EPS_C * log_total(scores, 1)


def coarse_blocks(pot_other, mass_other, cent_self, cent_other):
    count = cent_self.shape[1]
    width = math.gcd(count, 8)
    portions = cent_self.reshape(3, count // width, width).transpose(1, 0, 2)
    result = lax.map(
        lambda portion: coarse_update(pot_other, mass_other, portion, cent_other), portions
    )
    return result.reshape(count)


def merge_parts(first, second):
    highest = jnp.maximum(first[0], second[0])
    return (
        highest,
        first[1] * jnp.exp(first[0] - highest) + second[1] * jnp.exp(second[0] - highest),
    )


def column_partials(src_mass, src_pot, src_cent, cent_other):
    count = src_cent.shape[1]
    width = math.gcd(count, 8)
    cent_groups = src_cent.reshape(3, count // width, width).transpose(1, 0, 2)
    mass_groups = src_mass.reshape(count // width, width)
    pot_groups = src_pot.reshape(count // width, width)
    columns = cent_other.shape[1]
    start = (jnp.full((columns,), NEGATIVE, jnp.float32), jnp.zeros((columns,), jnp.float32))

    def step(carry, inputs):
        cent_group, mass_group, pot_group = inputs
        scores = (
            mass_group[:, None] + (pot_group[:, None] - coarse_cost(cent_group, cent_other)) / EPS_C
        )
        highest = jnp.max(scores, axis=0)
        summed = jnp.sum(jnp.exp(scores - highest[None, :]), axis=0)
        return (merge_parts(carry, (highest, summed)), None)

    result, unused = lax.scan(step, start, (cent_groups, mass_groups, pot_groups))
    return result


def pair_cost(src_group, tgt_group):
    distance = (src_group[:, 0, None, :, None] - tgt_group[:, 0, :, None, :]) ** 2
    distance = distance + (src_group[:, 1, None, :, None] - tgt_group[:, 1, :, None, :]) ** 2
    distance = distance + (src_group[:, 2, None, :, None] - tgt_group[:, 2, :, None, :]) ** 2
    return distance


def fine_rows(distance, tgt_mass, tgt_pot, usable):
    scores = tgt_mass[:, :, None, :] + (tgt_pot[:, :, None, :] - distance) / EPS_F
    scores = jnp.where(usable[:, :, None, None], scores, NEGATIVE)
    return -TAU_F * EPS_F * log_total(scores, (1, 3))


def fine_parts(distance, src_mass, src_pot, usable):
    scores = src_mass[:, None, :, None] + (src_pot[:, None, :, None] - distance) / EPS_F
    highest = jnp.max(scores, axis=2)
    summed = jnp.sum(jnp.exp(scores - highest[:, :, None, :]), axis=2)
    highest = jnp.where(usable[:, :, None], highest, NEGATIVE)
    summed = jnp.where(usable[:, :, None], summed, 0.0)
    return (highest, summed)


def local_exchanged(source_coords, target_coords, source_logmass, target_logmass, pair_targets, pair_counts):
    clusters = source_coords.shape[1]
    points = source_coords.shape[2]
    listed_slots = pair_targets.shape[1]
    row_count = lax.axis_size("rows")
    col_count = lax.axis_size("cols")
    own_index = lax.axis_index("rows") * col_count + lax.axis_index("cols")
    src_cent = jnp.mean(source_coords, axis=2)
    tgt_cent = jnp.mean(target_coords, axis=2)
    src_mass = log_total(source_logmass, 1)
    tgt_mass = log_total(target_logmass, 1)
    every_tgt = lax.all_gather(
        jnp.concatenate([tgt_cent, tgt_mass[None, :]], 0), ("rows", "cols"), axis=1, tiled=True
    )
    tgt_all = jnp.zeros((every_tgt.shape[1],), jnp.float32)
    for sweep in range(C_ITERS):
        src_own = coarse_blocks(tgt_all, every_tgt[3], src_cent, every_tgt[:3])
        highest, summed = column_partials(src_mass, src_own, src_cent, every_tgt[:3])
        highest, summed = joined((highest, summed), ("rows", "cols"), merge_parts)
        tgt_all = -TAU_C * EPS_C * (highest + jnp.log(summed))
    tgt_own = lax.dynamic_slice_in_dim(tgt_all, own_index * clusters, clusters)
    remote = listed_slots - 1
    capacity = 2 * -(-(clusters * remote) // (2 * (row_count - 1)))
    slot_total = row_count * capacity
    remote_ids = pair_targets[:, 1:]
    owner_row = remote_ids // clusters // col_count
    local_ids = remote_ids % clusters
    remote_used = jnp.arange(1, listed_slots)[None, :] < pair_counts[:, None]
    flat_rows = owner_row.reshape(-1)
    flat_used = remote_used.reshape(-1)
    onehot = ((flat_rows[:, None] == jnp.arange(row_count)[None, :]) & flat_used[:, None]).astype(
        jnp.int32
    )
    before = jnp.cumsum(onehot, axis=0) - onehot
    rank_of = jnp.sum(before * onehot, axis=1)
    slot_of = jnp.where(flat_used, flat_rows * capacity + rank_of, slot_total)
    requests = (
        jnp.full((slot_total,), -1, jnp.int32).at[slot_of].set(local_ids.reshape(-1), mode="drop")
    )
    asked = lax.all_to_all(
        requests.reshape(row_count, capacity), "rows", split_axis=0, concat_axis=0, tiled=True
    )
    asked_flat = asked.reshape(-1)
    asked_index = jnp.maximum(asked_flat, 0)
    own_table = jnp.concatenate([target_coords, target_logmass[None, :, :]], 0)
    sent_cells = own_table[:, asked_index].reshape(4, row_count, capacity, points)
    got_cells = lax.all_to_all(sent_cells, "rows", split_axis=1, concat_axis=1, tiled=True)
    cell_table = jnp.concatenate([own_table, got_cells.reshape(4, slot_total, points)], 1)
    pair_index = jnp.concatenate(
        [
            jnp.arange(clusters)[:, None],
            jnp.where(remote_used, clusters + slot_of.reshape(clusters, remote), 0),
        ],
        1,
    )
    pair_cells = cell_table[:, pair_index].transpose(1, 0, 2, 3)
    usable = jnp.arange(listed_slots)[None, :] < pair_counts[:, None]
    matches = jnp.arange(clusters)[:, None] == asked_flat[None, :]
    match_table = matches.astype(jnp.float32)
    group_size = math.gcd(clusters, 4)
    group_count = clusters // group_size

    def in_groups(array):
        return array.reshape((group_count, group_size) + array.shape[1:])

    src_sorted = source_coords.transpose(1, 0, 2)
    pair_mass = pair_cells[:, 3]
    fcost = lax.map(
        lambda inputs: pair_cost(inputs[0], inputs[1][:, :3]),
        (in_groups(src_sorted), in_groups(pair_cells)),
    )
    tgt_now = jnp.broadcast_to(tgt_own[:, None], (clusters, points))
    src_now = jnp.zeros((clusters, points), jnp.float32)
    for sweep in range(F_ITERS):
        sent_pot = tgt_now[asked_index].reshape(row_count, capacity, points)
        got_pot = lax.all_to_all(sent_pot, "rows", split_axis=0, concat_axis=0, tiled=True)
        pot_table = jnp.concatenate([tgt_now, got_pot.reshape(slot_total, points)], 0)
        pair_pot = pot_table[pair_index]

        def rows_of(inputs):
            cost_group, mass_group, pot_group, usable_now = inputs
            return fine_rows(cost_group, mass_group, pot_group, usable_now)

        src_now = lax.map(
            rows_of, (fcost, in_groups(pair_mass), in_groups(pair_pot), in_groups(usable))
        ).reshape(clusters, points)

        def parts_of(inputs):
            cost_group, mass_group, pot_group, usable_now = inputs
            return fine_parts(cost_group, mass_group, pot_group, usable_now)

        highs, sums = lax.map(
            parts_of, (fcost, in_groups(source_logmass), in_groups(src_now), in_groups(usable))
        )
        highs = highs.reshape(clusters, listed_slots, points)
        sums = sums.reshape(clusters, listed_slots, points)
        back_high = (
            jnp.full((slot_total, points), NEGATIVE, jnp.float32)
            .at[slot_of]
            .set(highs[:, 1:].reshape(-1, points), mode="drop")
        )
        back_sum = (
            jnp.zeros((slot_total, points), jnp.float32)
            .at[slot_of]
            .set(sums[:, 1:].reshape(-1, points), mode="drop")
        )
        got_high, got_sum = (
            lax.all_to_all(
                back_high.reshape(row_count, capacity, points),
                "rows",
                split_axis=0,
                concat_axis=0,
                tiled=True,
            ),
            lax.all_to_all(
                back_sum.reshape(row_count, capacity, points),
                "rows",
                split_axis=0,
                concat_axis=0,
                tiled=True,
            ),
        )
        got_high = got_high.reshape(slot_total, points)
        got_sum = got_sum.reshape(slot_total, points)
        best = jnp.maximum(
            highs[:, 0],
            jnp.max(jnp.where(matches[:, :, None], got_high[None, :, :], NEGATIVE), axis=1),
        )
        scaled = got_sum * jnp.exp(got_high - best[asked_index])
        combined = sums[:, 0] * jnp.exp(highs[:, 0] - best) + jnp.dot(
            match_table, scaled, precision=lax.Precision.HIGHEST
        )
        tgt_now = -TAU_F * EPS_F * (best + jnp.log(combined))
    return (src_now, tgt_now)


FEATURES = 32
CENTRE = 1.5
GROUP = 8
LOG2E = math.log2(math.e)
LN2 = math.log(2.0)


def three_parts(value):
    first = value.astype(jnp.bfloat16).astype(jnp.float32)
    left = value - first
    second = left.astype(jnp.bfloat16).astype(jnp.float32)
    return first, second, left - second


def coarse_start(stats):
    by_src = jnp.transpose(stats)
    cost = (by_src[:, 0:1] - stats[4:5]) ** 2
    cost = cost + (by_src[:, 1:2] - stats[5:6]) ** 2
    cost = (cost + (by_src[:, 2:3] - stats[6:7]) ** 2) / EPS_C
    return stats[7:8] - cost, by_src[:, 3:4] - cost


def coarse_sweep(to_src, to_tgt, tgt):
    scores = to_src + tgt / EPS_C
    highest = jnp.max(scores, axis=1, keepdims=True)
    summed = jnp.sum(jnp.exp(scores - highest), axis=1, keepdims=True)
    src = -TAU_C * EPS_C * (highest + jnp.log(summed))
    scores = to_tgt + src / EPS_C
    highest = jnp.max(scores, axis=0, keepdims=True)
    summed = jnp.sum(jnp.exp(scores - highest), axis=0, keepdims=True)
    return -TAU_C * EPS_C * (highest + jnp.log(summed))


def pack_kernel(src_coords, tgt_coords, src_logmass, tgt_logmass, listed, counts, out, blocks):
    own, points = src_logmass.shape
    slots = listed.shape[1]
    row = lax.axis_index("rows")
    col_count = lax.axis_size("cols")
    for axis in range(3):
        blocks[:, axis, :] = src_coords[axis]
        blocks[:, 4 + axis, :] = tgt_coords[axis]
    blocks[:, 3, :] = src_logmass[...]
    blocks[:, 7, :] = tgt_logmass[...]
    row_id = lax.broadcasted_iota(jnp.int32, (8, points), 0)
    lane = lax.broadcasted_iota(jnp.int32, (8, points), 1)
    known = jnp.zeros((8, points), jnp.float32)
    for q in range(own):
        block = blocks[q]
        highest = jnp.max(block, axis=1, keepdims=True)
        mass = highest + jnp.log(jnp.sum(jnp.exp(block - highest), axis=1, keepdims=True))
        mean = jnp.sum(block, axis=1, keepdims=True) / points
        value = jnp.where(row_id % 4 == 3, mass, mean)
        known = jnp.where(lane == row * own + q, value, known)
    pairs = own * slots
    for q in range(own):
        for k in range(slots):
            target = listed[q, k]
            place = target // (own * col_count) * own + target % own
            is_used = k < counts[q]
            at = pairs + q * slots + k
            known = jnp.where((row_id == row) & (lane == at), jnp.where(is_used, place, 0).astype(jnp.float32), known)
            known = jnp.where((row_id == row) & (lane == at + pairs), jnp.where(is_used, 1.0, 0.0), known)
    for peer in range(out.shape[0]):
        for q in range(own):
            out[peer, q] = blocks[q]
        out[peer, own] = known


def spread(bias, left, parts_ref):
    clusters, points = bias.shape
    for part, value in enumerate(three_parts(bias * LOG2E)):
        parts_ref[:, part, :] = value
    by_point = jnp.transpose(parts_ref[...].reshape(4 * clusters, points))
    for c in range(clusters):
        shift = (FEATURES - 8 - 4 * c) % (4 * clusters)
        moved = pltpu.roll(by_point, shift, 1) if shift else by_point
        left[c, :, FEATURES - 8 : FEATURES - 4] = moved[:, FEATURES - 8 : FEATURES - 4].astype(jnp.bfloat16)


def ready_kernel(
    packed, known_ref, src_right, tgt_right, src_left, tgt_left, src_rows, tgt_rows, owner, owner_row_ref, lists_ref, parts_ref,
):
    devices, blocks, _, points = packed.shape
    own = blocks - 1
    clusters = devices * own
    pairs = owner.shape[0]
    slots = pairs // clusters
    local_pairs = own * slots
    row_id = lax.broadcasted_iota(jnp.int32, (8, points), 0)
    lane_id = lax.broadcasted_iota(jnp.int32, (8, points), 1)
    row = lax.axis_index("rows")
    known = known_ref[...]

    for d in range(devices):
        rows = pl.ds(d * own, own)
        for into, base in ((src_rows, 0), (tgt_rows, 4)):
            into[0, rows, :] = packed[d, :own, base + 3, :]
            square = jnp.zeros((own, points), jnp.float32)
            for axis in range(3):
                square = square + (packed[d, :own, base + axis, :] - CENTRE) ** 2
            into[1, rows, :] = square / EPS_F
    by_lane = jnp.transpose(known)
    first_pair = lax.broadcasted_iota(jnp.int32, (1, points), 1)
    owner_row = [jnp.zeros((1, points), jnp.float32) for _ in range(pairs // points)]
    used = []
    per_row = points // local_pairs
    for d in range(devices):
        held = by_lane[local_pairs : 2 * local_pairs, d : d + 1]
        owner[pl.ds(d * local_pairs, local_pairs), :] = jnp.broadcast_to(held, (local_pairs, points))
        used.append(jnp.broadcast_to(by_lane[2 * local_pairs : 3 * local_pairs, d : d + 1], (local_pairs, points)))
        shift = (d % per_row * local_pairs - local_pairs) % points
        moved = pltpu.roll(known, shift, 1) if shift else known
        start = d % per_row * local_pairs
        inside = (first_pair >= start) & (first_pair < start + local_pairs)
        owner_row[d // per_row] = jnp.where(inside, moved[d : d + 1], owner_row[d // per_row])
    used = jnp.concatenate(used, 0)
    target = owner[...]
    low = (row * own).astype(jnp.float32)
    mine = jnp.where((target >= low) & (target < low + own), used, 0.0)
    of_source = jnp.max(mine.reshape(clusters, slots, points), axis=1, keepdims=True)
    needed = used * jnp.broadcast_to(of_source, (clusters, slots, points)).reshape(pairs, points)
    before = lax.broadcasted_iota(jnp.int32, (pairs, pairs), 1) <= lax.broadcasted_iota(jnp.int32, (pairs, pairs), 0)
    before = jnp.where(before, 1.0, 0.0).astype(jnp.bfloat16)
    known_of = jnp.concatenate(owner_row, 1)
    owner_row_ref[...] = known_of
    pair_id = lax.broadcasted_iota(jnp.int32, (8, pairs), 1).astype(jnp.float32)
    odd_row = lax.broadcasted_iota(jnp.int32, (8, pairs), 0) % 2 == 1
    pair_id = jnp.where(odd_row, known_of, pair_id).astype(jnp.bfloat16)
    place_id = lax.broadcasted_iota(jnp.int32, (pairs, points), 1).astype(jnp.float32) + 1.0
    lists_ref[...] = jnp.zeros(lists_ref.shape, jnp.int32)
    for which, mask in enumerate((used, needed, mine)):
        place = jnp.dot(before, mask.astype(jnp.bfloat16), preferred_element_type=jnp.float32)
        for part in range(pairs // points):
            hit = jnp.where(place == place_id + float(part * points), mask, 0.0).astype(jnp.bfloat16)
            order = jnp.dot(pair_id, hit, preferred_element_type=jnp.float32)
            lists_ref[2 * which : 2 * which + 2, pl.ds(part * points, points)] = order[:2].astype(jnp.int32)
        lists_ref[2 * which : 2 * which + 2, pl.ds(pairs, points)] = jnp.where(
            lane_id[:2] == points - 1, jnp.broadcast_to(place[pairs - 1 :], (2, points)), 0.0
        ).astype(jnp.int32)

    def features(coords, order):
        parts = three_parts(coords)
        groups = [parts[one] + jnp.roll(parts[two], 3, 0) for one, two in order]
        return jnp.concatenate(groups + [jnp.where(row_id < 3, 1.0, 0.0)], 0)

    def prepare(c):
        coords = jnp.where(row_id < 3, packed[lax.div(c, own), lax.rem(c, own)] - CENTRE, 0.0)
        wide = features(coords, ((0, 0), (1, 1), (0, 2)))
        src_right[c] = wide.astype(jnp.bfloat16)
        src_left[c] = jnp.transpose(wide).astype(jnp.bfloat16)
        coords = jnp.where(row_id < 3, (jnp.roll(packed[lax.div(c, own), lax.rem(c, own)], -4, 0) - CENTRE) * (2.0 / EPS_F * LOG2E), 0.0)
        wide = features(coords, ((0, 1), (0, 1), (2, 0)))
        tgt_right[c] = wide.astype(jnp.bfloat16)
        tgt_left[c] = jnp.transpose(wide).astype(jnp.bfloat16)

    def some(at, carry):
        for c in range(8):
            prepare(at * 8 + c)
        return carry

    lax.fori_loop(0, clusters // 8, some, 0)
    parts_ref[...] = jnp.zeros((clusters, 4, points), jnp.float32)
    spread(tgt_rows[0] - tgt_rows[1], tgt_left, parts_ref)


def fine_kernel(
    known, second, third, fourth, src_right, tgt_right, src_rows, tgt_rows, owner, owner_row, lists_ref, src_left_in, tgt_left_in,
    src_out, tgt_out, src_left, tgt_left,
    parts_ref, even, odd, highs, sums, src_pot, best_rows, to_src, to_tgt, lists, copied,
):
    move = pltpu.make_async_copy(lists_ref, lists, copied)
    move.start()
    clusters, points = src_pot.shape
    own = src_out.shape[0]
    pairs = highs.shape[0]
    slots = pairs // clusters
    lane_id = lax.broadcasted_iota(jnp.int32, (8, points), 1)
    row = lax.axis_index("rows")

    def pair_pass(which, by_target, beside=None):
        left, right = (src_left, tgt_right) if by_target else (tgt_left, src_right)

        steps = lax.div(lists[2 * which, pairs + points - 1] + (2 * GROUP - 1), 2 * GROUP)

        def score(group, lane, buffer):
            pair = lists[2 * which, group * GROUP + lane]
            src = lax.shift_right_logical(pair, slots.bit_length() - 1)
            tgt = lists[2 * which + 1, group * GROUP + lane]
            row, col = (src, tgt) if by_target else (tgt, src)
            buffer[lane] = jnp.dot(left[row], right[col], preferred_element_type=jnp.float32)

        def reduce(group, lane, buffer):
            pair = lists[2 * which, group * GROUP + lane]
            scores = buffer[lane]
            highest = jnp.max(scores, axis=0, keepdims=True)
            highs[pl.ds(pair, 1), :] = highest
            sums[pl.ds(pair, 1), :] = jnp.sum(jnp.exp2(scores - highest), axis=0, keepdims=True)

        def step(at, carry):
            for group, ready, filled in ((2 * at, even, odd), (2 * at + 1, odd, even)):
                for lane in range(GROUP):
                    score(group + 1, lane, filled)
                    reduce(group, lane, ready)
            return carry

        for lane in range(GROUP):
            score(0, lane, even)
        if beside is None:
            lax.fori_loop(0, steps, step, 0)
            return None

        def both(at, state):
            step(at, 0)
            return beside(state)

        state = lax.fori_loop(0, C_ITERS, both, jnp.zeros((1, points), jnp.float32))
        lax.fori_loop(C_ITERS, steps, step, 0)
        return state

    def by_pair(rows):
        lane = lax.broadcasted_iota(jnp.int32, (pairs, points), 1)
        picks = jnp.where((lane >= FEATURES) & ((lane % clusters).astype(jnp.float32) == owner[...]), 1.0, 0.0)
        parts = jnp.concatenate((jnp.zeros((FEATURES, points), jnp.float32),) + three_parts(rows), 0)
        return jnp.dot(picks.astype(jnp.bfloat16), parts.astype(jnp.bfloat16), preferred_element_type=jnp.float32)

    def src_update(high):
        high = high.reshape(clusters, slots, points)
        best = jnp.max(high, axis=1)
        total = jnp.sum(sums[...].reshape(clusters, slots, points) * jnp.exp2(high - best[:, None, :]), axis=1)
        value = -TAU_F * EPS_F * (LN2 * (best + jnp.log2(total)) - src_rows[1])
        src_pot[...] = value
        return src_rows[0] + value / EPS_F - src_rows[1]

    def best_of(t):
        return jnp.max(jnp.where(owner[...] == t.astype(jnp.float32), highs[...], NEGATIVE), axis=0, keepdims=True)

    def tgt_merge():
        width = math.gcd(clusters, 4)

        def find(at, carry):
            for step in range(width):
                best_rows[pl.ds(at * width + step, 1), :] = best_of(at * width + step)
            return carry

        lax.fori_loop(0, clusters // width, find, 0)
        best = best_rows[...]
        weighted = three_parts(sums[...] * jnp.exp2(highs[...] - by_pair(best)))
        number = lax.broadcasted_iota(jnp.int32, (clusters, pairs), 0)
        gather = jnp.where(number.astype(jnp.float32) == owner_row[...], 1.0, 0.0).astype(jnp.bfloat16)
        total = sum(
            jnp.dot(gather, part.astype(jnp.bfloat16), preferred_element_type=jnp.float32) for part in weighted
        )
        return LN2 * (best + jnp.log2(total))

    parts_ref[...] = jnp.zeros((clusters, 4, points), jnp.float32)
    highs[...] = jnp.full((pairs, points), NEGATIVE, jnp.float32)
    sums[...] = jnp.zeros((pairs, points), jnp.float32)
    stats = jnp.where(lane_id < clusters, known[...], 0.0)
    for away, other in enumerate((second, third, fourth), 1):
        inside = (lane_id >= away * clusters) & (lane_id < (away + 1) * clusters)
        stats = jnp.where(inside, pltpu.roll(other[...], away * clusters, 1), stats)
    to_src[...], to_tgt[...] = coarse_start(stats)
    move.wait()
    first_own = row * own
    coarse = pair_pass(0, False, lambda tgt: coarse_sweep(to_src[...], to_tgt[...], tgt))
    coarse = jnp.transpose(jnp.broadcast_to(coarse, (points, points)))[:clusters]
    spread(src_update(highs[...] + by_pair(coarse * (LOG2E / EPS_F))), src_left, parts_ref)
    for sweep in range(1, F_ITERS):
        pair_pass(0, True)
        value = -TAU_F * EPS_F * (tgt_merge() - tgt_rows[1])
        spread(tgt_rows[0] + value / EPS_F - tgt_rows[1], tgt_left, parts_ref)
        pair_pass(1 if sweep == F_ITERS - 1 else 0, False)
        spread(src_update(highs[...]), src_left, parts_ref)
    pair_pass(2, True)
    for c in range(own):
        t = first_own + c
        best = best_of(t)
        mine = jnp.where(owner[...] == t.astype(jnp.float32), sums[...] * jnp.exp2(highs[...] - best), 0.0)
        total = LN2 * (best + jnp.log2(jnp.sum(mine, axis=0, keepdims=True)))
        tgt_out[pl.ds(c, 1), :] = -TAU_F * EPS_F * (total - tgt_rows[1, pl.ds(t, 1), :])
        src_out[pl.ds(c, 1), :] = src_pot[pl.ds(t, 1), :]


def local_gathered(source_coords, target_coords, source_logmass, target_logmass, pair_targets, pair_counts):
    own, points = source_coords.shape[1:]
    slots = pair_targets.shape[1]
    row_count = lax.axis_size("rows")
    clusters = own * row_count
    pairs = clusters * slots
    whole = pl.BlockSpec(memory_space=pltpu.VMEM)
    scalars = pl.BlockSpec(memory_space=pltpu.SMEM)
    packed = pl.pallas_call(
        pack_kernel,
        out_shape=pltpu.VMEM((row_count, own + 1, 8, points), jnp.float32),
        in_specs=[whole] * 4 + [scalars] * 2,
        out_specs=whole,
        scratch_shapes=[pltpu.VMEM((own, 8, points), jnp.float32)],
        name="pack",
    )(source_coords, target_coords, source_logmass, target_logmass, pair_targets, pair_counts)
    packed = lax.all_to_all(packed, "rows", split_axis=0, concat_axis=0, tiled=True)
    known = [jnp.sum(packed[:, own], axis=0)]
    for away in range(1, 4):
        known.append(lax.ppermute(known[0], "cols", [(c, c ^ away) for c in range(4)]))
    features = jax.ShapeDtypeStruct((clusters, FEATURES, points), jnp.bfloat16)
    by_point = jax.ShapeDtypeStruct((clusters, points, FEATURES), jnp.bfloat16)
    rows = jax.ShapeDtypeStruct((2, clusters, points), jnp.float32)
    ready = pl.pallas_call(
        ready_kernel,
        out_shape=(
            features,
            features,
            by_point,
            by_point,
            rows,
            rows,
            jax.ShapeDtypeStruct((pairs, points), jnp.float32),
            jax.ShapeDtypeStruct((1, pairs), jnp.float32),
            jax.ShapeDtypeStruct((8, pairs + points), jnp.int32),
        ),
        in_specs=[whole] * 2,
        out_specs=(whole,) * 9,
        scratch_shapes=[pltpu.VMEM((clusters, 4, points), jnp.float32)],
        compiler_params=pltpu.CompilerParams(vmem_limit_bytes=12 * 2**20),
        cost_estimate=pl.CostEstimate(flops=4 * 10**6, bytes_accessed=4 * 10**6, transcendentals=0),
        name="ready",
    )(packed, known[0])
    src_right, tgt_right, src_left, tgt_left, src_rows, tgt_rows, owner, owner_row, lists = ready
    source, target, _, _ = pl.pallas_call(
        fine_kernel,
        out_shape=(jax.ShapeDtypeStruct((own, points), jnp.float32),) * 2 + (by_point,) * 2,
        in_specs=[whole] * 13,
        out_specs=(whole,) * 4,
        input_output_aliases={11: 2, 12: 3},
        scratch_shapes=[
            pltpu.VMEM((clusters, 4, points), jnp.float32),
            pltpu.VMEM((GROUP, points, points), jnp.float32),
            pltpu.VMEM((GROUP, points, points), jnp.float32),
            pltpu.VMEM((pairs, points), jnp.float32),
            pltpu.VMEM((pairs, points), jnp.float32),
            pltpu.VMEM((clusters, points), jnp.float32),
            pltpu.VMEM((clusters, points), jnp.float32),
            pltpu.VMEM((points, points), jnp.float32),
            pltpu.VMEM((points, points), jnp.float32),
            pltpu.SMEM((8, pairs + points), jnp.int32),
            pltpu.SemaphoreType.DMA(()),
        ],
        compiler_params=pltpu.CompilerParams(
            vmem_limit_bytes=12 * 2**20
        ),
        name="fine",
    )(*known, src_right, tgt_right, src_rows, tgt_rows, owner, owner_row, lists, src_left, tgt_left)
    return source, target


def solution(mesh):
    columns = mesh.shape["rows"]

    def local(*args):
        clusters, points = args[0].shape[1:]
        slots = args[4].shape[1]
        fits = clusters * columns * 4 == points and 3 * clusters * slots <= points and slots * columns * clusters % points == 0
        if mesh.shape["cols"] == 4 and columns == slots == 8 and clusters * slots == 32 and fits:
            return local_gathered(*args)
        return local_exchanged(*args)

    return jax.shard_map(
        local,
        mesh=mesh,
        in_specs=(
            P(None, ("rows", "cols"), None),
            P(None, ("rows", "cols"), None),
            P(("rows", "cols"), None),
            P(("rows", "cols"), None),
            P(("rows", "cols"), None),
            P(("rows", "cols")),
        ),
        out_specs=(P(("rows", "cols"), None), P(("rows", "cols"), None)),
        check_vma=False,
    )
```

```python
import math

import jax
import jax.numpy as jnp
from jax import lax
from jax.experimental import pallas as pl
from jax.experimental.pallas import tpu as pltpu
from jax.sharding import PartitionSpec as P

C_ITERS = 4
F_ITERS = 2


NEGATIVE = -1e30
EPS_C = 0.5
EPS_F = 0.1
RHO = 1.0
TAU_C = RHO / (RHO + EPS_C)
TAU_F = RHO / (RHO + EPS_F)


def joined(part, axis, combine):
    gathered = jax.tree.map(lambda a: lax.all_gather(a, axis), part)

    def take(source):
        return jax.tree.map(lambda a: lax.dynamic_index_in_dim(a, source, 0, False), gathered)

    return lax.fori_loop(
        1, lax.axis_size(axis), lambda source, state: combine(state, take(source)), take(0)
    )


def log_total(values, over_axes):
    highest = jnp.max(values, axis=over_axes, keepdims=True)
    summed = jnp.sum(jnp.exp(values - highest), axis=over_axes)
    return jnp.squeeze(highest, over_axes) + jnp.log(summed)


def coarse_cost(cent_self, cent_other):
    distance = (cent_self[0][:, None] - cent_other[0][None, :]) ** 2
    distance = distance + (cent_self[1][:, None] - cent_other[1][None, :]) ** 2
    distance = distance + (cent_self[2][:, None] - cent_other[2][None, :]) ** 2
    return distance


def coarse_update(pot_other, mass_other, cent_self, cent_other):
    scores = mass_other[None, :] + (pot_other[None, :] - coarse_cost(cent_self, cent_other)) / EPS_C
    return -TAU_C * EPS_C * log_total(scores, 1)


def coarse_blocks(pot_other, mass_other, cent_self, cent_other):
    count = cent_self.shape[1]
    width = math.gcd(count, 8)
    portions = cent_self.reshape(3, count // width, width).transpose(1, 0, 2)
    result = lax.map(
        lambda portion: coarse_update(pot_other, mass_other, portion, cent_other), portions
    )
    return result.reshape(count)


def merge_parts(first, second):
    highest = jnp.maximum(first[0], second[0])
    return (
        highest,
        first[1] * jnp.exp(first[0] - highest) + second[1] * jnp.exp(second[0] - highest),
    )


def column_partials(src_mass, src_pot, src_cent, cent_other):
    count = src_cent.shape[1]
    width = math.gcd(count, 8)
    cent_groups = src_cent.reshape(3, count // width, width).transpose(1, 0, 2)
    mass_groups = src_mass.reshape(count // width, width)
    pot_groups = src_pot.reshape(count // width, width)
    columns = cent_other.shape[1]
    start = (jnp.full((columns,), NEGATIVE, jnp.float32), jnp.zeros((columns,), jnp.float32))

    def step(carry, inputs):
        cent_group, mass_group, pot_group = inputs
        scores = (
            mass_group[:, None] + (pot_group[:, None] - coarse_cost(cent_group, cent_other)) / EPS_C
        )
        highest = jnp.max(scores, axis=0)
        summed = jnp.sum(jnp.exp(scores - highest[None, :]), axis=0)
        return (merge_parts(carry, (highest, summed)), None)

    result, unused = lax.scan(step, start, (cent_groups, mass_groups, pot_groups))
    return result


def pair_cost(src_group, tgt_group):
    distance = (src_group[:, 0, None, :, None] - tgt_group[:, 0, :, None, :]) ** 2
    distance = distance + (src_group[:, 1, None, :, None] - tgt_group[:, 1, :, None, :]) ** 2
    distance = distance + (src_group[:, 2, None, :, None] - tgt_group[:, 2, :, None, :]) ** 2
    return distance


def fine_rows(distance, tgt_mass, tgt_pot, usable):
    scores = tgt_mass[:, :, None, :] + (tgt_pot[:, :, None, :] - distance) / EPS_F
    scores = jnp.where(usable[:, :, None, None], scores, NEGATIVE)
    return -TAU_F * EPS_F * log_total(scores, (1, 3))


def fine_parts(distance, src_mass, src_pot, usable):
    scores = src_mass[:, None, :, None] + (src_pot[:, None, :, None] - distance) / EPS_F
    highest = jnp.max(scores, axis=2)
    summed = jnp.sum(jnp.exp(scores - highest[:, :, None, :]), axis=2)
    highest = jnp.where(usable[:, :, None], highest, NEGATIVE)
    summed = jnp.where(usable[:, :, None], summed, 0.0)
    return (highest, summed)


def local_exchanged(source_coords, target_coords, source_logmass, target_logmass, pair_targets, pair_counts):
    clusters = source_coords.shape[1]
    points = source_coords.shape[2]
    listed_slots = pair_targets.shape[1]
    row_count = lax.axis_size("rows")
    col_count = lax.axis_size("cols")
    own_index = lax.axis_index("rows") * col_count + lax.axis_index("cols")
    src_cent = jnp.mean(source_coords, axis=2)
    tgt_cent = jnp.mean(target_coords, axis=2)
    src_mass = log_total(source_logmass, 1)
    tgt_mass = log_total(target_logmass, 1)
    every_tgt = lax.all_gather(
        jnp.concatenate([tgt_cent, tgt_mass[None, :]], 0), ("rows", "cols"), axis=1, tiled=True
    )
    tgt_all = jnp.zeros((every_tgt.shape[1],), jnp.float32)
    for sweep in range(C_ITERS):
        src_own = coarse_blocks(tgt_all, every_tgt[3], src_cent, every_tgt[:3])
        highest, summed = column_partials(src_mass, src_own, src_cent, every_tgt[:3])
        highest, summed = joined((highest, summed), ("rows", "cols"), merge_parts)
        tgt_all = -TAU_C * EPS_C * (highest + jnp.log(summed))
    tgt_own = lax.dynamic_slice_in_dim(tgt_all, own_index * clusters, clusters)
    remote = listed_slots - 1
    capacity = 2 * -(-(clusters * remote) // (2 * (row_count - 1)))
    slot_total = row_count * capacity
    remote_ids = pair_targets[:, 1:]
    owner_row = remote_ids // clusters // col_count
    local_ids = remote_ids % clusters
    remote_used = jnp.arange(1, listed_slots)[None, :] < pair_counts[:, None]
    flat_rows = owner_row.reshape(-1)
    flat_used = remote_used.reshape(-1)
    onehot = ((flat_rows[:, None] == jnp.arange(row_count)[None, :]) & flat_used[:, None]).astype(
        jnp.int32
    )
    before = jnp.cumsum(onehot, axis=0) - onehot
    rank_of = jnp.sum(before * onehot, axis=1)
    slot_of = jnp.where(flat_used, flat_rows * capacity + rank_of, slot_total)
    requests = (
        jnp.full((slot_total,), -1, jnp.int32).at[slot_of].set(local_ids.reshape(-1), mode="drop")
    )
    asked = lax.all_to_all(
        requests.reshape(row_count, capacity), "rows", split_axis=0, concat_axis=0, tiled=True
    )
    asked_flat = asked.reshape(-1)
    asked_index = jnp.maximum(asked_flat, 0)
    own_table = jnp.concatenate([target_coords, target_logmass[None, :, :]], 0)
    sent_cells = own_table[:, asked_index].reshape(4, row_count, capacity, points)
    got_cells = lax.all_to_all(sent_cells, "rows", split_axis=1, concat_axis=1, tiled=True)
    cell_table = jnp.concatenate([own_table, got_cells.reshape(4, slot_total, points)], 1)
    pair_index = jnp.concatenate(
        [
            jnp.arange(clusters)[:, None],
            jnp.where(remote_used, clusters + slot_of.reshape(clusters, remote), 0),
        ],
        1,
    )
    pair_cells = cell_table[:, pair_index].transpose(1, 0, 2, 3)
    usable = jnp.arange(listed_slots)[None, :] < pair_counts[:, None]
    matches = jnp.arange(clusters)[:, None] == asked_flat[None, :]
    match_table = matches.astype(jnp.float32)
    group_size = math.gcd(clusters, 4)
    group_count = clusters // group_size

    def in_groups(array):
        return array.reshape((group_count, group_size) + array.shape[1:])

    src_sorted = source_coords.transpose(1, 0, 2)
    pair_mass = pair_cells[:, 3]
    fcost = lax.map(
        lambda inputs: pair_cost(inputs[0], inputs[1][:, :3]),
        (in_groups(src_sorted), in_groups(pair_cells)),
    )
    tgt_now = jnp.broadcast_to(tgt_own[:, None], (clusters, points))
    src_now = jnp.zeros((clusters, points), jnp.float32)
    for sweep in range(F_ITERS):
        sent_pot = tgt_now[asked_index].reshape(row_count, capacity, points)
        got_pot = lax.all_to_all(sent_pot, "rows", split_axis=0, concat_axis=0, tiled=True)
        pot_table = jnp.concatenate([tgt_now, got_pot.reshape(slot_total, points)], 0)
        pair_pot = pot_table[pair_index]

        def rows_of(inputs):
            cost_group, mass_group, pot_group, usable_now = inputs
            return fine_rows(cost_group, mass_group, pot_group, usable_now)

        src_now = lax.map(
            rows_of, (fcost, in_groups(pair_mass), in_groups(pair_pot), in_groups(usable))
        ).reshape(clusters, points)

        def parts_of(inputs):
            cost_group, mass_group, pot_group, usable_now = inputs
            return fine_parts(cost_group, mass_group, pot_group, usable_now)

        highs, sums = lax.map(
            parts_of, (fcost, in_groups(source_logmass), in_groups(src_now), in_groups(usable))
        )
        highs = highs.reshape(clusters, listed_slots, points)
        sums = sums.reshape(clusters, listed_slots, points)
        back_high = (
            jnp.full((slot_total, points), NEGATIVE, jnp.float32)
            .at[slot_of]
            .set(highs[:, 1:].reshape(-1, points), mode="drop")
        )
        back_sum = (
            jnp.zeros((slot_total, points), jnp.float32)
            .at[slot_of]
            .set(sums[:, 1:].reshape(-1, points), mode="drop")
        )
        got_high, got_sum = (
            lax.all_to_all(
                back_high.reshape(row_count, capacity, points),
                "rows",
                split_axis=0,
                concat_axis=0,
                tiled=True,
            ),
            lax.all_to_all(
                back_sum.reshape(row_count, capacity, points),
                "rows",
                split_axis=0,
                concat_axis=0,
                tiled=True,
            ),
        )
        got_high = got_high.reshape(slot_total, points)
        got_sum = got_sum.reshape(slot_total, points)
        best = jnp.maximum(
            highs[:, 0],
            jnp.max(jnp.where(matches[:, :, None], got_high[None, :, :], NEGATIVE), axis=1),
        )
        scaled = got_sum * jnp.exp(got_high - best[asked_index])
        combined = sums[:, 0] * jnp.exp(highs[:, 0] - best) + jnp.dot(
            match_table, scaled, precision=lax.Precision.HIGHEST
        )
        tgt_now = -TAU_F * EPS_F * (best + jnp.log(combined))
    return (src_now, tgt_now)


FEATURES = 32
CENTRE = 1.5
GROUP = 64
REST = 32
FIRST = 32
LOG2E = math.log2(math.e)
LN2 = math.log(2.0)


def three_parts(value):
    first = value.astype(jnp.bfloat16).astype(jnp.float32)
    left = value - first
    second = left.astype(jnp.bfloat16).astype(jnp.float32)
    return first, second, left - second


def coarse_start(stats):
    by_src = jnp.transpose(stats)
    cost = (by_src[:, 0:1] - stats[4:5]) ** 2
    cost = cost + (by_src[:, 1:2] - stats[5:6]) ** 2
    cost = (cost + (by_src[:, 2:3] - stats[6:7]) ** 2) / EPS_C
    return stats[7:8] - cost, by_src[:, 3:4] - cost


def coarse_sweep(to_src, to_tgt, tgt):
    scores = to_src + tgt / EPS_C
    highest = jnp.max(scores, axis=1, keepdims=True)
    summed = jnp.sum(jnp.exp(scores - highest), axis=1, keepdims=True)
    src = -TAU_C * EPS_C * (highest + jnp.log(summed))
    scores = to_tgt + src / EPS_C
    highest = jnp.max(scores, axis=0, keepdims=True)
    summed = jnp.sum(jnp.exp(scores - highest), axis=0, keepdims=True)
    return -TAU_C * EPS_C * (highest + jnp.log(summed))


def pack_kernel(src_coords, tgt_coords, src_logmass, tgt_logmass, listed, counts, out, blocks):
    own, points = src_logmass.shape
    slots = listed.shape[1]
    row = lax.axis_index("rows")
    col_count = lax.axis_size("cols")
    for axis in range(3):
        blocks[:, axis, :] = src_coords[axis]
        blocks[:, 4 + axis, :] = tgt_coords[axis]
    blocks[:, 3, :] = src_logmass[...]
    blocks[:, 7, :] = tgt_logmass[...]
    row_id = lax.broadcasted_iota(jnp.int32, (8, points), 0)
    lane = lax.broadcasted_iota(jnp.int32, (8, points), 1)
    known = jnp.zeros((8, points), jnp.float32)
    for q in range(own):
        block = blocks[q]
        highest = jnp.max(block, axis=1, keepdims=True)
        mass = highest + jnp.log(jnp.sum(jnp.exp(block - highest), axis=1, keepdims=True))
        mean = jnp.sum(block, axis=1, keepdims=True) / points
        value = jnp.where(row_id % 4 == 3, mass, mean)
        known = jnp.where(lane == row * own + q, value, known)
    pairs = own * slots
    for q in range(own):
        for k in range(slots):
            target = listed[q, k]
            place = target // (own * col_count) * own + target % own
            is_used = k < counts[q]
            at = pairs + q * slots + k
            known = jnp.where((row_id == row) & (lane == at), jnp.where(is_used, place, 0).astype(jnp.float32), known)
            known = jnp.where((row_id == row) & (lane == at + pairs), jnp.where(is_used, 1.0, 0.0), known)
    for q in range(own):
        out[q] = blocks[q]
    out[own] = known


def spread(bias, left, parts_ref):
    clusters, points = bias.shape
    for part, value in enumerate(three_parts(bias * LOG2E)):
        parts_ref[:, part, :] = value
    by_point = jnp.transpose(parts_ref[...].reshape(4 * clusters, points))
    for c in range(0, clusters, 2):
        shift = (FEATURES - 8 - 4 * c) % (4 * clusters)
        moved = (pltpu.roll(by_point, shift, 1) if shift else by_point).astype(jnp.bfloat16)
        left[c, :, FEATURES - 8 : FEATURES - 4] = moved[:, FEATURES - 8 : FEATURES - 4]
        left[c + 1, :, FEATURES - 4 : FEATURES] = moved[:, FEATURES - 4 : FEATURES]


def ready_kernel(
    near, far, known_ref, src_right, tgt_right, src_left, tgt_left, src_rows, tgt_rows, owner, owner_row_ref, lists_ref, parts_ref,
):
    clusters, points = src_rows.shape[1:]
    devices = known_ref.shape[0]
    own = clusters // devices
    half = devices // 2
    pairs = owner.shape[0]
    slots = pairs // clusters
    local_pairs = own * slots
    row_id = lax.broadcasted_iota(jnp.int32, (8, points), 0)
    lane_id = lax.broadcasted_iota(jnp.int32, (8, points), 1)
    row = lax.axis_index("rows")
    known = known_ref[...]

    for away in range(devices):
        held = near if away < half else far
        at = away % half * (own + 1)
        rows = pl.ds(lax.bitwise_xor(row, away) * own, own)
        for into, base in ((src_rows, 0), (tgt_rows, 4)):
            into[0, rows, :] = held[at : at + own, base + 3, :]
            square = jnp.zeros((own, points), jnp.float32)
            for axis in range(3):
                square = square + (held[at : at + own, base + axis, :] - CENTRE) ** 2
            into[1, rows, :] = square / EPS_F
    by_lane = jnp.transpose(known)
    first_pair = lax.broadcasted_iota(jnp.int32, (1, points), 1)
    owner_row = [jnp.zeros((1, points), jnp.float32) for _ in range(pairs // points)]
    used = []
    per_row = points // local_pairs
    for d in range(devices):
        held = by_lane[local_pairs : 2 * local_pairs, d : d + 1]
        owner[pl.ds(d * local_pairs, local_pairs), :] = jnp.broadcast_to(held, (local_pairs, points))
        used.append(jnp.broadcast_to(by_lane[2 * local_pairs : 3 * local_pairs, d : d + 1], (local_pairs, points)))
        shift = (d % per_row * local_pairs - local_pairs) % points
        moved = pltpu.roll(known, shift, 1) if shift else known
        start = d % per_row * local_pairs
        inside = (first_pair >= start) & (first_pair < start + local_pairs)
        owner_row[d // per_row] = jnp.where(inside, moved[d : d + 1], owner_row[d // per_row])
    used = jnp.concatenate(used, 0)
    target = owner[...]
    low = (row * own).astype(jnp.float32)
    mine = jnp.where((target >= low) & (target < low + own), used, 0.0)
    of_source = jnp.max(mine.reshape(clusters, slots, points), axis=1, keepdims=True)
    needed = used * jnp.broadcast_to(of_source, (clusters, slots, points)).reshape(pairs, points)
    before = lax.broadcasted_iota(jnp.int32, (pairs, pairs), 1) <= lax.broadcasted_iota(jnp.int32, (pairs, pairs), 0)
    before = jnp.where(before, 1.0, 0.0).astype(jnp.bfloat16)
    known_of = jnp.concatenate(owner_row, 1)
    owner_row_ref[...] = known_of
    pair_id = lax.broadcasted_iota(jnp.int32, (8, pairs), 1).astype(jnp.float32)
    odd_row = lax.broadcasted_iota(jnp.int32, (8, pairs), 0) % 2 == 1
    pair_id = jnp.where(odd_row, known_of, pair_id).astype(jnp.bfloat16)
    place_id = lax.broadcasted_iota(jnp.int32, (pairs, points), 1).astype(jnp.float32) + 1.0
    lists_ref[...] = jnp.zeros(lists_ref.shape, jnp.int32)
    for which, mask in enumerate((used, needed, mine)):
        place = jnp.dot(before, mask.astype(jnp.bfloat16), preferred_element_type=jnp.float32)
        for part in range(pairs // points):
            hit = jnp.where(place == place_id + float(part * points), mask, 0.0).astype(jnp.bfloat16)
            order = jnp.dot(pair_id, hit, preferred_element_type=jnp.float32)
            lists_ref[2 * which : 2 * which + 2, pl.ds(part * points, points)] = order[:2].astype(jnp.int32)
        lists_ref[2 * which : 2 * which + 2, pl.ds(pairs, points)] = jnp.where(
            lane_id[:2] == points - 1, jnp.broadcast_to(place[pairs - 1 :], (2, points)), 0.0
        ).astype(jnp.int32)

    picked = jnp.where(row_id % 4 < 3, 1.0, 0.0)
    none = jnp.zeros((8, points), jnp.float32)

    def prepare(c, coords, order, right, left):
        parts = three_parts(coords)
        groups = [parts[one] + jnp.roll(parts[two], 3, 0) for one, two in order]
        right[c] = jnp.concatenate(groups + [picked], 0).astype(jnp.bfloat16)
        left[c] = jnp.transpose(jnp.concatenate(groups + [none], 0)).astype(jnp.bfloat16)

    def some(at, carry):
        for held, first in ((near, 0), (far, half)):
            for q in range(own):
                block = held[at * (own + 1) + q]
                c = lax.bitwise_xor(row, at + first) * own + q
                coords = jnp.where(row_id < 3, block - CENTRE, 0.0)
                prepare(c, coords, ((0, 0), (1, 1), (0, 2)), src_right, src_left)
                coords = jnp.where(row_id < 3, (jnp.roll(block, -4, 0) - CENTRE) * (2.0 / EPS_F * LOG2E), 0.0)
                prepare(c, coords, ((0, 1), (0, 1), (2, 0)), tgt_right, tgt_left)
        return carry

    lax.fori_loop(0, half, some, 0)
    parts_ref[...] = jnp.zeros((clusters, 4, points), jnp.float32)
    spread(tgt_rows[0] - tgt_rows[1], tgt_left, parts_ref)


def fine_kernel(
    known, second, third, fourth, src_right, tgt_right, src_rows, tgt_rows, owner, owner_row, lists_ref, src_left_in, tgt_left_in,
    src_out, tgt_out, src_left, tgt_left,
    parts_ref, highs, sums, src_pot, best_rows, to_src, to_tgt, lists, copied,
):
    move = pltpu.make_async_copy(lists_ref, lists, copied)
    move.start()
    clusters, points = src_pot.shape
    own = src_out.shape[0]
    pairs = highs.shape[0]
    slots = pairs // clusters
    lane_id = lax.broadcasted_iota(jnp.int32, (8, points), 1)
    row = lax.axis_index("rows")

    def pair_pass(which, by_target, beside=None):
        left, right = (src_left, tgt_right) if by_target else (tgt_left, src_right)

        count = lists[2 * which, pairs + points - 1]

        def some(start, size):
            for lane in range(size):
                pair = lists[2 * which, start + lane]
                src = lax.shift_right_logical(pair, slots.bit_length() - 1)
                tgt = lists[2 * which + 1, start + lane]
                row, col = (src, tgt) if by_target else (tgt, src)
                scores = jnp.dot(left[row], right[col], preferred_element_type=jnp.float32)
                highest = jnp.max(scores, axis=0, keepdims=True)
                highs[pl.ds(pair, 1), :] = highest
                sums[pl.ds(pair, 1), :] = jnp.sum(jnp.exp2(scores - highest), axis=0, keepdims=True)

        state, done = None, 0
        if beside is not None:

            def both(at, state):
                some(at * FIRST, FIRST)
                return beside(state)

            state = lax.fori_loop(0, C_ITERS, both, jnp.zeros((1, points), jnp.float32))
            done = C_ITERS * FIRST

        def many(at, carry):
            some(done + at * GROUP, GROUP)
            return carry

        def few(at, carry):
            some(at * REST, REST)
            return carry

        if which < 2:
            steps = jnp.maximum(lax.div(count - done, GROUP), 0)
            lax.fori_loop(0, steps, many, 0)
            done = done + steps * GROUP

        lax.fori_loop(lax.div(done, REST), lax.div(count + (REST - 1), REST), few, 0)
        return state

    def by_pair(rows):
        lane = lax.broadcasted_iota(jnp.int32, (pairs, points), 1)
        picks = jnp.where((lane >= FEATURES) & ((lane % clusters).astype(jnp.float32) == owner[...]), 1.0, 0.0)
        parts = jnp.concatenate((jnp.zeros((FEATURES, points), jnp.float32),) + three_parts(rows), 0)
        return jnp.dot(picks.astype(jnp.bfloat16), parts.astype(jnp.bfloat16), preferred_element_type=jnp.float32)

    def src_update(high):
        high = high.reshape(clusters, slots, points)
        best = jnp.max(high, axis=1)
        total = jnp.sum(sums[...].reshape(clusters, slots, points) * jnp.exp2(high - best[:, None, :]), axis=1)
        value = -TAU_F * EPS_F * (LN2 * (best + jnp.log2(total)) - src_rows[1])
        src_pot[...] = value
        return src_rows[0] + value / EPS_F - src_rows[1]

    def best_of(t):
        return jnp.max(jnp.where(owner[...] == t.astype(jnp.float32), highs[...], NEGATIVE), axis=0, keepdims=True)

    def tgt_merge():
        width = math.gcd(clusters, 4)

        def find(at, carry):
            for step in range(width):
                best_rows[pl.ds(at * width + step, 1), :] = best_of(at * width + step)
            return carry

        lax.fori_loop(0, clusters // width, find, 0)
        best = best_rows[...]
        weighted = three_parts(sums[...] * jnp.exp2(highs[...] - by_pair(best)))
        number = lax.broadcasted_iota(jnp.int32, (clusters, pairs), 0)
        gather = jnp.where(number.astype(jnp.float32) == owner_row[...], 1.0, 0.0).astype(jnp.bfloat16)
        total = sum(
            jnp.dot(gather, part.astype(jnp.bfloat16), preferred_element_type=jnp.float32) for part in weighted
        )
        return LN2 * (best + jnp.log2(total))

    parts_ref[...] = jnp.zeros((clusters, 4, points), jnp.float32)
    highs[...] = jnp.full((pairs, points), NEGATIVE, jnp.float32)
    sums[...] = jnp.zeros((pairs, points), jnp.float32)
    stats = jnp.where(lane_id < clusters, known[...], 0.0)
    for away, other in enumerate((second, third, fourth), 1):
        inside = (lane_id >= away * clusters) & (lane_id < (away + 1) * clusters)
        stats = jnp.where(inside, pltpu.roll(other[...], away * clusters, 1), stats)
    to_src[...], to_tgt[...] = coarse_start(stats)
    move.wait()
    first_own = row * own
    coarse = pair_pass(0, False, lambda tgt: coarse_sweep(to_src[...], to_tgt[...], tgt))
    coarse = jnp.transpose(jnp.broadcast_to(coarse, (points, points)))[:clusters]
    spread(src_update(highs[...] + by_pair(coarse * (LOG2E / EPS_F))), src_left, parts_ref)
    for sweep in range(1, F_ITERS):
        pair_pass(0, True)
        value = -TAU_F * EPS_F * (tgt_merge() - tgt_rows[1])
        spread(tgt_rows[0] + value / EPS_F - tgt_rows[1], tgt_left, parts_ref)
        pair_pass(1 if sweep == F_ITERS - 1 else 0, False)
        spread(src_update(highs[...]), src_left, parts_ref)
    pair_pass(2, True)
    for c in range(own):
        t = first_own + c
        best = best_of(t)
        mine = jnp.where(owner[...] == t.astype(jnp.float32), sums[...] * jnp.exp2(highs[...] - best), 0.0)
        total = LN2 * (best + jnp.log2(jnp.sum(mine, axis=0, keepdims=True)))
        tgt_out[pl.ds(c, 1), :] = -TAU_F * EPS_F * (total - tgt_rows[1, pl.ds(t, 1), :])
        src_out[pl.ds(c, 1), :] = src_pot[pl.ds(t, 1), :]


def local_gathered(source_coords, target_coords, source_logmass, target_logmass, pair_targets, pair_counts):
    own, points = source_coords.shape[1:]
    slots = pair_targets.shape[1]
    row_count = lax.axis_size("rows")
    clusters = own * row_count
    pairs = clusters * slots
    whole = pl.BlockSpec(memory_space=pltpu.VMEM)
    scalars = pl.BlockSpec(memory_space=pltpu.SMEM)
    packed = pl.pallas_call(
        pack_kernel,
        out_shape=pltpu.VMEM((own + 1, 8, points), jnp.float32),
        in_specs=[whole] * 4 + [scalars] * 2,
        out_specs=whole,
        scratch_shapes=[pltpu.VMEM((own, 8, points), jnp.float32)],
        name="pack",
    )(source_coords, target_coords, source_logmass, target_logmass, pair_targets, pair_counts)

    def from_row(value, away):
        return lax.ppermute(value, "rows", [(r, r ^ away) for r in range(row_count)])

    near = jnp.concatenate([packed] + [from_row(packed, away) for away in range(1, 4)], 0)
    far = from_row(near, 4)
    held = jnp.stack([near, far]).reshape(row_count, own + 1, 8, points)
    known = [jnp.sum(held[:, own], axis=0)]
    for away in range(1, 4):
        known.append(lax.ppermute(known[0], "cols", [(c, c ^ away) for c in range(4)]))
    features = jax.ShapeDtypeStruct((clusters, FEATURES, points), jnp.bfloat16)
    by_point = jax.ShapeDtypeStruct((clusters, points, FEATURES), jnp.bfloat16)
    rows = jax.ShapeDtypeStruct((2, clusters, points), jnp.float32)
    ready = pl.pallas_call(
        ready_kernel,
        out_shape=(
            features,
            features,
            by_point,
            by_point,
            rows,
            rows,
            jax.ShapeDtypeStruct((pairs, points), jnp.float32),
            jax.ShapeDtypeStruct((1, pairs), jnp.float32),
            jax.ShapeDtypeStruct((8, pairs + points), jnp.int32),
        ),
        in_specs=[whole] * 3,
        out_specs=(whole,) * 9,
        scratch_shapes=[pltpu.VMEM((clusters, 4, points), jnp.float32)],
        compiler_params=pltpu.CompilerParams(vmem_limit_bytes=12 * 2**20),
        cost_estimate=pl.CostEstimate(flops=4 * 10**6, bytes_accessed=4 * 10**6, transcendentals=0),
        name="ready",
    )(near, far, known[0])
    src_right, tgt_right, src_left, tgt_left, src_rows, tgt_rows, owner, owner_row, lists = ready
    source, target, _, _ = pl.pallas_call(
        fine_kernel,
        out_shape=(jax.ShapeDtypeStruct((own, points), jnp.float32),) * 2 + (by_point,) * 2,
        in_specs=[whole] * 13,
        out_specs=(whole,) * 4,
        input_output_aliases={11: 2, 12: 3},
        scratch_shapes=[
            pltpu.VMEM((clusters, 4, points), jnp.float32),
            pltpu.VMEM((pairs, points), jnp.float32),
            pltpu.VMEM((pairs, points), jnp.float32),
            pltpu.VMEM((clusters, points), jnp.float32),
            pltpu.VMEM((clusters, points), jnp.float32),
            pltpu.VMEM((points, points), jnp.float32),
            pltpu.VMEM((points, points), jnp.float32),
            pltpu.SMEM((8, pairs + points), jnp.int32),
            pltpu.SemaphoreType.DMA(()),
        ],
        compiler_params=pltpu.CompilerParams(
            vmem_limit_bytes=12 * 2**20
        ),
        name="fine",
    )(*known, src_right, tgt_right, src_rows, tgt_rows, owner, owner_row, lists, src_left, tgt_left)
    return source, target


def solution(mesh):
    columns = mesh.shape["rows"]

    def local(*args):
        clusters, points = args[0].shape[1:]
        slots = args[4].shape[1]
        fits = clusters * columns * 4 == points and 3 * clusters * slots <= points and slots * columns * clusters % points == 0
        if mesh.shape["cols"] == 4 and columns == slots == 8 and clusters * slots == 32 and fits:
            return local_gathered(*args)
        return local_exchanged(*args)

    return jax.shard_map(
        local,
        mesh=mesh,
        in_specs=(
            P(None, ("rows", "cols"), None),
            P(None, ("rows", "cols"), None),
            P(("rows", "cols"), None),
            P(("rows", "cols"), None),
            P(("rows", "cols"), None),
            P(("rows", "cols")),
        ),
        out_specs=(P(("rows", "cols"), None), P(("rows", "cols"), None)),
        check_vma=False,
    )
```

```python
import math

import jax
import jax.numpy as jnp
from jax import lax
from jax.experimental import pallas as pl
from jax.experimental.pallas import tpu as pltpu
from jax.sharding import PartitionSpec as P

C_ITERS = 4
F_ITERS = 2


NEGATIVE = -1e30
EPS_C = 0.5
EPS_F = 0.1
RHO = 1.0
TAU_C = RHO / (RHO + EPS_C)
TAU_F = RHO / (RHO + EPS_F)


def joined(part, axis, combine):
    gathered = jax.tree.map(lambda a: lax.all_gather(a, axis), part)

    def take(source):
        return jax.tree.map(lambda a: lax.dynamic_index_in_dim(a, source, 0, False), gathered)

    return lax.fori_loop(
        1, lax.axis_size(axis), lambda source, state: combine(state, take(source)), take(0)
    )


def log_total(values, over_axes):
    highest = jnp.max(values, axis=over_axes, keepdims=True)
    summed = jnp.sum(jnp.exp(values - highest), axis=over_axes)
    return jnp.squeeze(highest, over_axes) + jnp.log(summed)


def coarse_cost(cent_self, cent_other):
    distance = (cent_self[0][:, None] - cent_other[0][None, :]) ** 2
    distance = distance + (cent_self[1][:, None] - cent_other[1][None, :]) ** 2
    distance = distance + (cent_self[2][:, None] - cent_other[2][None, :]) ** 2
    return distance


def coarse_update(pot_other, mass_other, cent_self, cent_other):
    scores = mass_other[None, :] + (pot_other[None, :] - coarse_cost(cent_self, cent_other)) / EPS_C
    return -TAU_C * EPS_C * log_total(scores, 1)


def coarse_blocks(pot_other, mass_other, cent_self, cent_other):
    count = cent_self.shape[1]
    width = math.gcd(count, 8)
    portions = cent_self.reshape(3, count // width, width).transpose(1, 0, 2)
    result = lax.map(
        lambda portion: coarse_update(pot_other, mass_other, portion, cent_other), portions
    )
    return result.reshape(count)


def merge_parts(first, second):
    highest = jnp.maximum(first[0], second[0])
    return (
        highest,
        first[1] * jnp.exp(first[0] - highest) + second[1] * jnp.exp(second[0] - highest),
    )


def column_partials(src_mass, src_pot, src_cent, cent_other):
    count = src_cent.shape[1]
    width = math.gcd(count, 8)
    cent_groups = src_cent.reshape(3, count // width, width).transpose(1, 0, 2)
    mass_groups = src_mass.reshape(count // width, width)
    pot_groups = src_pot.reshape(count // width, width)
    columns = cent_other.shape[1]
    start = (jnp.full((columns,), NEGATIVE, jnp.float32), jnp.zeros((columns,), jnp.float32))

    def step(carry, inputs):
        cent_group, mass_group, pot_group = inputs
        scores = (
            mass_group[:, None] + (pot_group[:, None] - coarse_cost(cent_group, cent_other)) / EPS_C
        )
        highest = jnp.max(scores, axis=0)
        summed = jnp.sum(jnp.exp(scores - highest[None, :]), axis=0)
        return (merge_parts(carry, (highest, summed)), None)

    result, unused = lax.scan(step, start, (cent_groups, mass_groups, pot_groups))
    return result


def pair_cost(src_group, tgt_group):
    distance = (src_group[:, 0, None, :, None] - tgt_group[:, 0, :, None, :]) ** 2
    distance = distance + (src_group[:, 1, None, :, None] - tgt_group[:, 1, :, None, :]) ** 2
    distance = distance + (src_group[:, 2, None, :, None] - tgt_group[:, 2, :, None, :]) ** 2
    return distance


def fine_rows(distance, tgt_mass, tgt_pot, usable):
    scores = tgt_mass[:, :, None, :] + (tgt_pot[:, :, None, :] - distance) / EPS_F
    scores = jnp.where(usable[:, :, None, None], scores, NEGATIVE)
    return -TAU_F * EPS_F * log_total(scores, (1, 3))


def fine_parts(distance, src_mass, src_pot, usable):
    scores = src_mass[:, None, :, None] + (src_pot[:, None, :, None] - distance) / EPS_F
    highest = jnp.max(scores, axis=2)
    summed = jnp.sum(jnp.exp(scores - highest[:, :, None, :]), axis=2)
    highest = jnp.where(usable[:, :, None], highest, NEGATIVE)
    summed = jnp.where(usable[:, :, None], summed, 0.0)
    return (highest, summed)


def local_exchanged(source_coords, target_coords, source_logmass, target_logmass, pair_targets, pair_counts):
    clusters = source_coords.shape[1]
    points = source_coords.shape[2]
    listed_slots = pair_targets.shape[1]
    row_count = lax.axis_size("rows")
    col_count = lax.axis_size("cols")
    own_index = lax.axis_index("rows") * col_count + lax.axis_index("cols")
    src_cent = jnp.mean(source_coords, axis=2)
    tgt_cent = jnp.mean(target_coords, axis=2)
    src_mass = log_total(source_logmass, 1)
    tgt_mass = log_total(target_logmass, 1)
    every_tgt = lax.all_gather(
        jnp.concatenate([tgt_cent, tgt_mass[None, :]], 0), ("rows", "cols"), axis=1, tiled=True
    )
    tgt_all = jnp.zeros((every_tgt.shape[1],), jnp.float32)
    for sweep in range(C_ITERS):
        src_own = coarse_blocks(tgt_all, every_tgt[3], src_cent, every_tgt[:3])
        highest, summed = column_partials(src_mass, src_own, src_cent, every_tgt[:3])
        highest, summed = joined((highest, summed), ("rows", "cols"), merge_parts)
        tgt_all = -TAU_C * EPS_C * (highest + jnp.log(summed))
    tgt_own = lax.dynamic_slice_in_dim(tgt_all, own_index * clusters, clusters)
    remote = listed_slots - 1
    capacity = 2 * -(-(clusters * remote) // (2 * (row_count - 1)))
    slot_total = row_count * capacity
    remote_ids = pair_targets[:, 1:]
    owner_row = remote_ids // clusters // col_count
    local_ids = remote_ids % clusters
    remote_used = jnp.arange(1, listed_slots)[None, :] < pair_counts[:, None]
    flat_rows = owner_row.reshape(-1)
    flat_used = remote_used.reshape(-1)
    onehot = ((flat_rows[:, None] == jnp.arange(row_count)[None, :]) & flat_used[:, None]).astype(
        jnp.int32
    )
    before = jnp.cumsum(onehot, axis=0) - onehot
    rank_of = jnp.sum(before * onehot, axis=1)
    slot_of = jnp.where(flat_used, flat_rows * capacity + rank_of, slot_total)
    requests = (
        jnp.full((slot_total,), -1, jnp.int32).at[slot_of].set(local_ids.reshape(-1), mode="drop")
    )
    asked = lax.all_to_all(
        requests.reshape(row_count, capacity), "rows", split_axis=0, concat_axis=0, tiled=True
    )
    asked_flat = asked.reshape(-1)
    asked_index = jnp.maximum(asked_flat, 0)
    own_table = jnp.concatenate([target_coords, target_logmass[None, :, :]], 0)
    sent_cells = own_table[:, asked_index].reshape(4, row_count, capacity, points)
    got_cells = lax.all_to_all(sent_cells, "rows", split_axis=1, concat_axis=1, tiled=True)
    cell_table = jnp.concatenate([own_table, got_cells.reshape(4, slot_total, points)], 1)
    pair_index = jnp.concatenate(
        [
            jnp.arange(clusters)[:, None],
            jnp.where(remote_used, clusters + slot_of.reshape(clusters, remote), 0),
        ],
        1,
    )
    pair_cells = cell_table[:, pair_index].transpose(1, 0, 2, 3)
    usable = jnp.arange(listed_slots)[None, :] < pair_counts[:, None]
    matches = jnp.arange(clusters)[:, None] == asked_flat[None, :]
    match_table = matches.astype(jnp.float32)
    group_size = math.gcd(clusters, 4)
    group_count = clusters // group_size

    def in_groups(array):
        return array.reshape((group_count, group_size) + array.shape[1:])

    src_sorted = source_coords.transpose(1, 0, 2)
    pair_mass = pair_cells[:, 3]
    fcost = lax.map(
        lambda inputs: pair_cost(inputs[0], inputs[1][:, :3]),
        (in_groups(src_sorted), in_groups(pair_cells)),
    )
    tgt_now = jnp.broadcast_to(tgt_own[:, None], (clusters, points))
    src_now = jnp.zeros((clusters, points), jnp.float32)
    for sweep in range(F_ITERS):
        sent_pot = tgt_now[asked_index].reshape(row_count, capacity, points)
        got_pot = lax.all_to_all(sent_pot, "rows", split_axis=0, concat_axis=0, tiled=True)
        pot_table = jnp.concatenate([tgt_now, got_pot.reshape(slot_total, points)], 0)
        pair_pot = pot_table[pair_index]

        def rows_of(inputs):
            cost_group, mass_group, pot_group, usable_now = inputs
            return fine_rows(cost_group, mass_group, pot_group, usable_now)

        src_now = lax.map(
            rows_of, (fcost, in_groups(pair_mass), in_groups(pair_pot), in_groups(usable))
        ).reshape(clusters, points)

        def parts_of(inputs):
            cost_group, mass_group, pot_group, usable_now = inputs
            return fine_parts(cost_group, mass_group, pot_group, usable_now)

        highs, sums = lax.map(
            parts_of, (fcost, in_groups(source_logmass), in_groups(src_now), in_groups(usable))
        )
        highs = highs.reshape(clusters, listed_slots, points)
        sums = sums.reshape(clusters, listed_slots, points)
        back_high = (
            jnp.full((slot_total, points), NEGATIVE, jnp.float32)
            .at[slot_of]
            .set(highs[:, 1:].reshape(-1, points), mode="drop")
        )
        back_sum = (
            jnp.zeros((slot_total, points), jnp.float32)
            .at[slot_of]
            .set(sums[:, 1:].reshape(-1, points), mode="drop")
        )
        got_high, got_sum = (
            lax.all_to_all(
                back_high.reshape(row_count, capacity, points),
                "rows",
                split_axis=0,
                concat_axis=0,
                tiled=True,
            ),
            lax.all_to_all(
                back_sum.reshape(row_count, capacity, points),
                "rows",
                split_axis=0,
                concat_axis=0,
                tiled=True,
            ),
        )
        got_high = got_high.reshape(slot_total, points)
        got_sum = got_sum.reshape(slot_total, points)
        best = jnp.maximum(
            highs[:, 0],
            jnp.max(jnp.where(matches[:, :, None], got_high[None, :, :], NEGATIVE), axis=1),
        )
        scaled = got_sum * jnp.exp(got_high - best[asked_index])
        combined = sums[:, 0] * jnp.exp(highs[:, 0] - best) + jnp.dot(
            match_table, scaled, precision=lax.Precision.HIGHEST
        )
        tgt_now = -TAU_F * EPS_F * (best + jnp.log(combined))
    return (src_now, tgt_now)


FEATURES = 32
CENTRE = 1.5
GROUP = 64
REST = 32
FIRST = 64
LOG2E = math.log2(math.e)
LN2 = math.log(2.0)


def three_parts(value):
    first = value.astype(jnp.bfloat16).astype(jnp.float32)
    left = value - first
    second = left.astype(jnp.bfloat16).astype(jnp.float32)
    return first, second, left - second


def coarse_start(stats):
    by_src = jnp.transpose(stats)
    cost = (by_src[:, 0:1] - stats[4:5]) ** 2
    cost = cost + (by_src[:, 1:2] - stats[5:6]) ** 2
    cost = (cost + (by_src[:, 2:3] - stats[6:7]) ** 2) / EPS_C
    return stats[7:8] - cost, by_src[:, 3:4] - cost


def coarse_sweep(to_src, to_tgt, tgt):
    scores = to_src + tgt / EPS_C
    highest = jnp.max(scores, axis=1, keepdims=True)
    summed = jnp.sum(jnp.exp(scores - highest), axis=1, keepdims=True)
    src = -TAU_C * EPS_C * (highest + jnp.log(summed))
    scores = to_tgt + src / EPS_C
    highest = jnp.max(scores, axis=0, keepdims=True)
    summed = jnp.sum(jnp.exp(scores - highest), axis=0, keepdims=True)
    return -TAU_C * EPS_C * (highest + jnp.log(summed))


def pack_kernel(src_coords, tgt_coords, src_logmass, tgt_logmass, listed, counts, out, blocks):
    own, points = src_logmass.shape
    slots = listed.shape[1]
    row = lax.axis_index("rows")
    col_count = lax.axis_size("cols")
    for axis in range(3):
        blocks[:, axis, :] = src_coords[axis]
        blocks[:, 4 + axis, :] = tgt_coords[axis]
    blocks[:, 3, :] = src_logmass[...]
    blocks[:, 7, :] = tgt_logmass[...]
    row_id = lax.broadcasted_iota(jnp.int32, (8, points), 0)
    lane = lax.broadcasted_iota(jnp.int32, (8, points), 1)
    known = jnp.zeros((8, points), jnp.float32)
    for q in range(own):
        block = blocks[q]
        highest = jnp.max(block, axis=1, keepdims=True)
        mass = highest + jnp.log(jnp.sum(jnp.exp(block - highest), axis=1, keepdims=True))
        mean = jnp.sum(block, axis=1, keepdims=True) / points
        value = jnp.where(row_id % 4 == 3, mass, mean)
        known = jnp.where(lane == row * own + q, value, known)
    pairs = own * slots
    for q in range(own):
        for k in range(slots):
            target = listed[q, k]
            place = target // (own * col_count) * own + target % own
            is_used = k < counts[q]
            at = pairs + q * slots + k
            known = jnp.where((row_id == row) & (lane == at), jnp.where(is_used, place, 0).astype(jnp.float32), known)
            known = jnp.where((row_id == row) & (lane == at + pairs), jnp.where(is_used, 1.0, 0.0), known)
    for q in range(own):
        out[q] = blocks[q]
    out[own] = known


def spread(bias, left, parts_ref):
    clusters, points = bias.shape
    for part, value in enumerate(three_parts(bias * LOG2E)):
        parts_ref[:, part, :] = value
    by_point = jnp.transpose(parts_ref[...].reshape(4 * clusters, points))
    for c in range(0, clusters, 2):
        shift = (FEATURES - 8 - 4 * c) % (4 * clusters)
        moved = (pltpu.roll(by_point, shift, 1) if shift else by_point).astype(jnp.bfloat16)
        left[c, :, FEATURES - 8 : FEATURES - 4] = moved[:, FEATURES - 8 : FEATURES - 4]
        left[c + 1, :, FEATURES - 4 : FEATURES] = moved[:, FEATURES - 4 : FEATURES]


def ready_kernel(
    near, far, known_ref, src_right, tgt_right, src_left, tgt_left, src_rows, tgt_rows, owner, owner_row_ref, lists_ref, parts_ref,
):
    clusters, points = src_rows.shape[1:]
    devices = known_ref.shape[0]
    own = clusters // devices
    half = devices // 2
    pairs = owner.shape[0]
    slots = pairs // clusters
    local_pairs = own * slots
    row_id = lax.broadcasted_iota(jnp.int32, (8, points), 0)
    lane_id = lax.broadcasted_iota(jnp.int32, (8, points), 1)
    row = lax.axis_index("rows")
    known = known_ref[...]

    for away in range(devices):
        held = near if away < half else far
        at = away % half * (own + 1)
        rows = pl.ds(lax.bitwise_xor(row, away) * own, own)
        for into, base in ((src_rows, 0), (tgt_rows, 4)):
            into[0, rows, :] = held[at : at + own, base + 3, :]
            square = jnp.zeros((own, points), jnp.float32)
            for axis in range(3):
                square = square + (held[at : at + own, base + axis, :] - CENTRE) ** 2
            into[1, rows, :] = square / EPS_F
    by_lane = jnp.transpose(known)
    first_pair = lax.broadcasted_iota(jnp.int32, (1, points), 1)
    owner_row = [jnp.zeros((1, points), jnp.float32) for _ in range(pairs // points)]
    used = []
    per_row = points // local_pairs
    for d in range(devices):
        held = by_lane[local_pairs : 2 * local_pairs, d : d + 1]
        owner[pl.ds(d * local_pairs, local_pairs), :] = jnp.broadcast_to(held, (local_pairs, points))
        used.append(jnp.broadcast_to(by_lane[2 * local_pairs : 3 * local_pairs, d : d + 1], (local_pairs, points)))
        shift = (d % per_row * local_pairs - local_pairs) % points
        moved = pltpu.roll(known, shift, 1) if shift else known
        start = d % per_row * local_pairs
        inside = (first_pair >= start) & (first_pair < start + local_pairs)
        owner_row[d // per_row] = jnp.where(inside, moved[d : d + 1], owner_row[d // per_row])
    used = jnp.concatenate(used, 0)
    target = owner[...]
    low = (row * own).astype(jnp.float32)
    mine = jnp.where((target >= low) & (target < low + own), used, 0.0)
    of_source = jnp.max(mine.reshape(clusters, slots, points), axis=1, keepdims=True)
    needed = used * jnp.broadcast_to(of_source, (clusters, slots, points)).reshape(pairs, points)
    before = lax.broadcasted_iota(jnp.int32, (pairs, pairs), 1) <= lax.broadcasted_iota(jnp.int32, (pairs, pairs), 0)
    before = jnp.where(before, 1.0, 0.0).astype(jnp.bfloat16)
    known_of = jnp.concatenate(owner_row, 1)
    owner_row_ref[...] = known_of
    pair_id = lax.broadcasted_iota(jnp.int32, (8, pairs), 1).astype(jnp.float32)
    odd_row = lax.broadcasted_iota(jnp.int32, (8, pairs), 0) % 2 == 1
    pair_id = jnp.where(odd_row, known_of, pair_id).astype(jnp.bfloat16)
    place_id = lax.broadcasted_iota(jnp.int32, (pairs, points), 1).astype(jnp.float32) + 1.0
    lists_ref[...] = jnp.zeros(lists_ref.shape, jnp.int32)
    for which, mask in enumerate((used, needed, mine)):
        place = jnp.dot(before, mask.astype(jnp.bfloat16), preferred_element_type=jnp.float32)
        for part in range(pairs // points):
            hit = jnp.where(place == place_id + float(part * points), mask, 0.0).astype(jnp.bfloat16)
            order = jnp.dot(pair_id, hit, preferred_element_type=jnp.float32)
            lists_ref[2 * which : 2 * which + 2, pl.ds(part * points, points)] = order[:2].astype(jnp.int32)
        lists_ref[2 * which : 2 * which + 2, pl.ds(pairs, points)] = jnp.where(
            lane_id[:2] == points - 1, jnp.broadcast_to(place[pairs - 1 :], (2, points)), 0.0
        ).astype(jnp.int32)

    picked = jnp.where(row_id % 4 < 3, 1.0, 0.0)
    none = jnp.zeros((8, points), jnp.float32)

    def prepare(c, coords, order, right, left):
        parts = three_parts(coords)
        groups = [parts[one] + jnp.roll(parts[two], 3, 0) for one, two in order]
        right[c] = jnp.concatenate(groups + [picked], 0).astype(jnp.bfloat16)
        left[c] = jnp.transpose(jnp.concatenate(groups + [none], 0)).astype(jnp.bfloat16)

    def some(at, carry):
        for held, first in ((near, 0), (far, half)):
            for q in range(own):
                block = held[at * (own + 1) + q]
                c = lax.bitwise_xor(row, at + first) * own + q
                coords = jnp.where(row_id < 3, block - CENTRE, 0.0)
                prepare(c, coords, ((0, 0), (1, 1), (0, 2)), src_right, src_left)
                coords = jnp.where(row_id < 3, (jnp.roll(block, -4, 0) - CENTRE) * (2.0 / EPS_F * LOG2E), 0.0)
                prepare(c, coords, ((0, 1), (0, 1), (2, 0)), tgt_right, tgt_left)
        return carry

    lax.fori_loop(0, half, some, 0)
    parts_ref[...] = jnp.zeros((clusters, 4, points), jnp.float32)
    spread(tgt_rows[0] - tgt_rows[1], tgt_left, parts_ref)


def fine_kernel(
    known, second, third, fourth, src_right, tgt_right, src_rows, tgt_rows, owner, owner_row, lists_ref, src_left_in, tgt_left_in,
    src_out, tgt_out, src_left, tgt_left,
    parts_ref, highs, sums, src_pot, best_rows, to_src, to_tgt, lists, copied,
):
    move = pltpu.make_async_copy(lists_ref, lists, copied)
    move.start()
    clusters, points = src_pot.shape
    own = src_out.shape[0]
    pairs = highs.shape[0]
    slots = pairs // clusters
    lane_id = lax.broadcasted_iota(jnp.int32, (8, points), 1)
    row = lax.axis_index("rows")

    def pair_pass(which, by_target, beside=None):
        left, right = (src_left, tgt_right) if by_target else (tgt_left, src_right)

        count = lists[2 * which, pairs + points - 1]

        def some(start, size):
            for lane in range(size):
                pair = lists[2 * which, start + lane]
                src = lax.shift_right_logical(pair, slots.bit_length() - 1)
                tgt = lists[2 * which + 1, start + lane]
                row, col = (src, tgt) if by_target else (tgt, src)
                scores = jnp.dot(left[row], right[col], preferred_element_type=jnp.float32)
                highest = jnp.max(scores, axis=0, keepdims=True)
                highs[pl.ds(pair, 1), :] = highest
                sums[pl.ds(pair, 1), :] = jnp.sum(jnp.exp2(scores - highest), axis=0, keepdims=True)

        state, done = None, 0
        if beside is not None:

            def both(at, state):
                some(at * FIRST, FIRST)
                return beside(beside(state))

            state = lax.fori_loop(0, C_ITERS // 2, both, jnp.zeros((1, points), jnp.float32))
            done = C_ITERS // 2 * FIRST

        def many(at, carry):
            some(done + at * GROUP, GROUP)
            return carry

        def few(at, carry):
            some(at * REST, REST)
            return carry

        if which < 2:
            steps = jnp.maximum(lax.div(count - done, GROUP), 0)
            lax.fori_loop(0, steps, many, 0)
            done = done + steps * GROUP

        lax.fori_loop(lax.div(done, REST), lax.div(count + (REST - 1), REST), few, 0)
        return state

    def by_pair(rows):
        lane = lax.broadcasted_iota(jnp.int32, (pairs, points), 1)
        picks = jnp.where((lane >= FEATURES) & ((lane % clusters).astype(jnp.float32) == owner[...]), 1.0, 0.0)
        parts = jnp.concatenate((jnp.zeros((FEATURES, points), jnp.float32),) + three_parts(rows), 0)
        return jnp.dot(picks.astype(jnp.bfloat16), parts.astype(jnp.bfloat16), preferred_element_type=jnp.float32)

    def src_update(high):
        high = high.reshape(clusters, slots, points)
        best = jnp.max(high, axis=1)
        total = jnp.sum(sums[...].reshape(clusters, slots, points) * jnp.exp2(high - best[:, None, :]), axis=1)
        value = -TAU_F * EPS_F * (LN2 * (best + jnp.log2(total)) - src_rows[1])
        src_pot[...] = value
        return src_rows[0] + value / EPS_F - src_rows[1]

    def best_of(t):
        return jnp.max(jnp.where(owner[...] == t.astype(jnp.float32), highs[...], NEGATIVE), axis=0, keepdims=True)

    def tgt_merge():
        width = math.gcd(clusters, 4)

        def find(at, carry):
            for step in range(width):
                best_rows[pl.ds(at * width + step, 1), :] = best_of(at * width + step)
            return carry

        lax.fori_loop(0, clusters // width, find, 0)
        best = best_rows[...]
        weighted = three_parts(sums[...] * jnp.exp2(highs[...] - by_pair(best)))
        number = lax.broadcasted_iota(jnp.int32, (clusters, pairs), 0)
        gather = jnp.where(number.astype(jnp.float32) == owner_row[...], 1.0, 0.0).astype(jnp.bfloat16)
        total = sum(
            jnp.dot(gather, part.astype(jnp.bfloat16), preferred_element_type=jnp.float32) for part in weighted
        )
        return LN2 * (best + jnp.log2(total))

    parts_ref[...] = jnp.zeros((clusters, 4, points), jnp.float32)
    highs[...] = jnp.full((pairs, points), NEGATIVE, jnp.float32)
    sums[...] = jnp.zeros((pairs, points), jnp.float32)
    stats = jnp.where(lane_id < clusters, known[...], 0.0)
    for away, other in enumerate((second, third, fourth), 1):
        inside = (lane_id >= away * clusters) & (lane_id < (away + 1) * clusters)
        stats = jnp.where(inside, pltpu.roll(other[...], away * clusters, 1), stats)
    to_src[...], to_tgt[...] = coarse_start(stats)
    move.wait()
    first_own = row * own
    coarse = pair_pass(0, False, lambda tgt: coarse_sweep(to_src[...], to_tgt[...], tgt))
    coarse = jnp.transpose(jnp.broadcast_to(coarse, (points, points)))[:clusters]
    spread(src_update(highs[...] + by_pair(coarse * (LOG2E / EPS_F))), src_left, parts_ref)
    for sweep in range(1, F_ITERS):
        pair_pass(0, True)
        value = -TAU_F * EPS_F * (tgt_merge() - tgt_rows[1])
        spread(tgt_rows[0] + value / EPS_F - tgt_rows[1], tgt_left, parts_ref)
        pair_pass(1 if sweep == F_ITERS - 1 else 0, False)
        spread(src_update(highs[...]), src_left, parts_ref)
    pair_pass(2, True)
    for c in range(own):
        t = first_own + c
        best = best_of(t)
        mine = jnp.where(owner[...] == t.astype(jnp.float32), sums[...] * jnp.exp2(highs[...] - best), 0.0)
        total = LN2 * (best + jnp.log2(jnp.sum(mine, axis=0, keepdims=True)))
        tgt_out[pl.ds(c, 1), :] = -TAU_F * EPS_F * (total - tgt_rows[1, pl.ds(t, 1), :])
        src_out[pl.ds(c, 1), :] = src_pot[pl.ds(t, 1), :]


def local_gathered(source_coords, target_coords, source_logmass, target_logmass, pair_targets, pair_counts):
    own, points = source_coords.shape[1:]
    slots = pair_targets.shape[1]
    row_count = lax.axis_size("rows")
    clusters = own * row_count
    pairs = clusters * slots
    whole = pl.BlockSpec(memory_space=pltpu.VMEM)
    scalars = pl.BlockSpec(memory_space=pltpu.SMEM)
    packed = pl.pallas_call(
        pack_kernel,
        out_shape=pltpu.VMEM((own + 1, 8, points), jnp.float32),
        in_specs=[whole] * 4 + [scalars] * 2,
        out_specs=whole,
        scratch_shapes=[pltpu.VMEM((own, 8, points), jnp.float32)],
        name="pack",
    )(source_coords, target_coords, source_logmass, target_logmass, pair_targets, pair_counts)

    def from_row(value, away):
        return lax.ppermute(value, "rows", [(r, r ^ away) for r in range(row_count)])

    near = jnp.concatenate([packed] + [from_row(packed, away) for away in range(1, 4)], 0)
    far = from_row(near, 4)
    held = jnp.stack([near, far]).reshape(row_count, own + 1, 8, points)
    known = [jnp.sum(held[:, own], axis=0)]
    for away in range(1, 4):
        known.append(lax.ppermute(known[0], "cols", [(c, c ^ away) for c in range(4)]))
    features = jax.ShapeDtypeStruct((clusters, FEATURES, points), jnp.bfloat16)
    by_point = jax.ShapeDtypeStruct((clusters, points, FEATURES), jnp.bfloat16)
    rows = jax.ShapeDtypeStruct((2, clusters, points), jnp.float32)
    ready = pl.pallas_call(
        ready_kernel,
        out_shape=(
            features,
            features,
            by_point,
            by_point,
            rows,
            rows,
            jax.ShapeDtypeStruct((pairs, points), jnp.float32),
            jax.ShapeDtypeStruct((1, pairs), jnp.float32),
            jax.ShapeDtypeStruct((8, pairs + points), jnp.int32),
        ),
        in_specs=[whole] * 3,
        out_specs=(whole,) * 9,
        scratch_shapes=[pltpu.VMEM((clusters, 4, points), jnp.float32)],
        compiler_params=pltpu.CompilerParams(vmem_limit_bytes=12 * 2**20),
        cost_estimate=pl.CostEstimate(flops=4 * 10**6, bytes_accessed=4 * 10**6, transcendentals=0),
        name="ready",
    )(near, far, known[0])
    src_right, tgt_right, src_left, tgt_left, src_rows, tgt_rows, owner, owner_row, lists = ready
    source, target, _, _ = pl.pallas_call(
        fine_kernel,
        out_shape=(jax.ShapeDtypeStruct((own, points), jnp.float32),) * 2 + (by_point,) * 2,
        in_specs=[whole] * 13,
        out_specs=(whole,) * 4,
        input_output_aliases={11: 2, 12: 3},
        scratch_shapes=[
            pltpu.VMEM((clusters, 4, points), jnp.float32),
            pltpu.VMEM((pairs, points), jnp.float32),
            pltpu.VMEM((pairs, points), jnp.float32),
            pltpu.VMEM((clusters, points), jnp.float32),
            pltpu.VMEM((clusters, points), jnp.float32),
            pltpu.VMEM((points, points), jnp.float32),
            pltpu.VMEM((points, points), jnp.float32),
            pltpu.SMEM((8, pairs + points), jnp.int32),
            pltpu.SemaphoreType.DMA(()),
        ],
        compiler_params=pltpu.CompilerParams(
            vmem_limit_bytes=12 * 2**20
        ),
        name="fine",
    )(*known, src_right, tgt_right, src_rows, tgt_rows, owner, owner_row, lists, src_left, tgt_left)
    return source, target


def solution(mesh):
    columns = mesh.shape["rows"]

    def local(*args):
        clusters, points = args[0].shape[1:]
        slots = args[4].shape[1]
        fits = clusters * columns * 4 == points and 3 * clusters * slots <= points and slots * columns * clusters % points == 0
        if mesh.shape["cols"] == 4 and columns == slots == 8 and clusters * slots == 32 and fits:
            return local_gathered(*args)
        return local_exchanged(*args)

    return jax.shard_map(
        local,
        mesh=mesh,
        in_specs=(
            P(None, ("rows", "cols"), None),
            P(None, ("rows", "cols"), None),
            P(("rows", "cols"), None),
            P(("rows", "cols"), None),
            P(("rows", "cols"), None),
            P(("rows", "cols")),
        ),
        out_specs=(P(("rows", "cols"), None), P(("rows", "cols"), None)),
        check_vma=False,
    )
```

```python
import math

import jax
import jax.numpy as jnp
from jax import lax
from jax.experimental import pallas as pl
from jax.experimental.pallas import tpu as pltpu
from jax.sharding import PartitionSpec as P

C_ITERS = 4
F_ITERS = 2


NEGATIVE = -1e30
EPS_C = 0.5
EPS_F = 0.1
RHO = 1.0
TAU_C = RHO / (RHO + EPS_C)
TAU_F = RHO / (RHO + EPS_F)


def joined(part, axis, combine):
    gathered = jax.tree.map(lambda a: lax.all_gather(a, axis), part)

    def take(source):
        return jax.tree.map(lambda a: lax.dynamic_index_in_dim(a, source, 0, False), gathered)

    return lax.fori_loop(
        1, lax.axis_size(axis), lambda source, state: combine(state, take(source)), take(0)
    )


def log_total(values, over_axes):
    highest = jnp.max(values, axis=over_axes, keepdims=True)
    summed = jnp.sum(jnp.exp(values - highest), axis=over_axes)
    return jnp.squeeze(highest, over_axes) + jnp.log(summed)


def coarse_cost(cent_self, cent_other):
    distance = (cent_self[0][:, None] - cent_other[0][None, :]) ** 2
    distance = distance + (cent_self[1][:, None] - cent_other[1][None, :]) ** 2
    distance = distance + (cent_self[2][:, None] - cent_other[2][None, :]) ** 2
    return distance


def coarse_update(pot_other, mass_other, cent_self, cent_other):
    scores = mass_other[None, :] + (pot_other[None, :] - coarse_cost(cent_self, cent_other)) / EPS_C
    return -TAU_C * EPS_C * log_total(scores, 1)


def coarse_blocks(pot_other, mass_other, cent_self, cent_other):
    count = cent_self.shape[1]
    width = math.gcd(count, 8)
    portions = cent_self.reshape(3, count // width, width).transpose(1, 0, 2)
    result = lax.map(
        lambda portion: coarse_update(pot_other, mass_other, portion, cent_other), portions
    )
    return result.reshape(count)


def merge_parts(first, second):
    highest = jnp.maximum(first[0], second[0])
    return (
        highest,
        first[1] * jnp.exp(first[0] - highest) + second[1] * jnp.exp(second[0] - highest),
    )


def column_partials(src_mass, src_pot, src_cent, cent_other):
    count = src_cent.shape[1]
    width = math.gcd(count, 8)
    cent_groups = src_cent.reshape(3, count // width, width).transpose(1, 0, 2)
    mass_groups = src_mass.reshape(count // width, width)
    pot_groups = src_pot.reshape(count // width, width)
    columns = cent_other.shape[1]
    start = (jnp.full((columns,), NEGATIVE, jnp.float32), jnp.zeros((columns,), jnp.float32))

    def step(carry, inputs):
        cent_group, mass_group, pot_group = inputs
        scores = (
            mass_group[:, None] + (pot_group[:, None] - coarse_cost(cent_group, cent_other)) / EPS_C
        )
        highest = jnp.max(scores, axis=0)
        summed = jnp.sum(jnp.exp(scores - highest[None, :]), axis=0)
        return (merge_parts(carry, (highest, summed)), None)

    result, unused = lax.scan(step, start, (cent_groups, mass_groups, pot_groups))
    return result


def pair_cost(src_group, tgt_group):
    distance = (src_group[:, 0, None, :, None] - tgt_group[:, 0, :, None, :]) ** 2
    distance = distance + (src_group[:, 1, None, :, None] - tgt_group[:, 1, :, None, :]) ** 2
    distance = distance + (src_group[:, 2, None, :, None] - tgt_group[:, 2, :, None, :]) ** 2
    return distance


def fine_rows(distance, tgt_mass, tgt_pot, usable):
    scores = tgt_mass[:, :, None, :] + (tgt_pot[:, :, None, :] - distance) / EPS_F
    scores = jnp.where(usable[:, :, None, None], scores, NEGATIVE)
    return -TAU_F * EPS_F * log_total(scores, (1, 3))


def fine_parts(distance, src_mass, src_pot, usable):
    scores = src_mass[:, None, :, None] + (src_pot[:, None, :, None] - distance) / EPS_F
    highest = jnp.max(scores, axis=2)
    summed = jnp.sum(jnp.exp(scores - highest[:, :, None, :]), axis=2)
    highest = jnp.where(usable[:, :, None], highest, NEGATIVE)
    summed = jnp.where(usable[:, :, None], summed, 0.0)
    return (highest, summed)


def local_exchanged(source_coords, target_coords, source_logmass, target_logmass, pair_targets, pair_counts):
    clusters = source_coords.shape[1]
    points = source_coords.shape[2]
    listed_slots = pair_targets.shape[1]
    row_count = lax.axis_size("rows")
    col_count = lax.axis_size("cols")
    own_index = lax.axis_index("rows") * col_count + lax.axis_index("cols")
    src_cent = jnp.mean(source_coords, axis=2)
    tgt_cent = jnp.mean(target_coords, axis=2)
    src_mass = log_total(source_logmass, 1)
    tgt_mass = log_total(target_logmass, 1)
    every_tgt = lax.all_gather(
        jnp.concatenate([tgt_cent, tgt_mass[None, :]], 0), ("rows", "cols"), axis=1, tiled=True
    )
    tgt_all = jnp.zeros((every_tgt.shape[1],), jnp.float32)
    for sweep in range(C_ITERS):
        src_own = coarse_blocks(tgt_all, every_tgt[3], src_cent, every_tgt[:3])
        highest, summed = column_partials(src_mass, src_own, src_cent, every_tgt[:3])
        highest, summed = joined((highest, summed), ("rows", "cols"), merge_parts)
        tgt_all = -TAU_C * EPS_C * (highest + jnp.log(summed))
    tgt_own = lax.dynamic_slice_in_dim(tgt_all, own_index * clusters, clusters)
    remote = listed_slots - 1
    capacity = 2 * -(-(clusters * remote) // (2 * (row_count - 1)))
    slot_total = row_count * capacity
    remote_ids = pair_targets[:, 1:]
    owner_row = remote_ids // clusters // col_count
    local_ids = remote_ids % clusters
    remote_used = jnp.arange(1, listed_slots)[None, :] < pair_counts[:, None]
    flat_rows = owner_row.reshape(-1)
    flat_used = remote_used.reshape(-1)
    onehot = ((flat_rows[:, None] == jnp.arange(row_count)[None, :]) & flat_used[:, None]).astype(
        jnp.int32
    )
    before = jnp.cumsum(onehot, axis=0) - onehot
    rank_of = jnp.sum(before * onehot, axis=1)
    slot_of = jnp.where(flat_used, flat_rows * capacity + rank_of, slot_total)
    requests = (
        jnp.full((slot_total,), -1, jnp.int32).at[slot_of].set(local_ids.reshape(-1), mode="drop")
    )
    asked = lax.all_to_all(
        requests.reshape(row_count, capacity), "rows", split_axis=0, concat_axis=0, tiled=True
    )
    asked_flat = asked.reshape(-1)
    asked_index = jnp.maximum(asked_flat, 0)
    own_table = jnp.concatenate([target_coords, target_logmass[None, :, :]], 0)
    sent_cells = own_table[:, asked_index].reshape(4, row_count, capacity, points)
    got_cells = lax.all_to_all(sent_cells, "rows", split_axis=1, concat_axis=1, tiled=True)
    cell_table = jnp.concatenate([own_table, got_cells.reshape(4, slot_total, points)], 1)
    pair_index = jnp.concatenate(
        [
            jnp.arange(clusters)[:, None],
            jnp.where(remote_used, clusters + slot_of.reshape(clusters, remote), 0),
        ],
        1,
    )
    pair_cells = cell_table[:, pair_index].transpose(1, 0, 2, 3)
    usable = jnp.arange(listed_slots)[None, :] < pair_counts[:, None]
    matches = jnp.arange(clusters)[:, None] == asked_flat[None, :]
    match_table = matches.astype(jnp.float32)
    group_size = math.gcd(clusters, 4)
    group_count = clusters // group_size

    def in_groups(array):
        return array.reshape((group_count, group_size) + array.shape[1:])

    src_sorted = source_coords.transpose(1, 0, 2)
    pair_mass = pair_cells[:, 3]
    fcost = lax.map(
        lambda inputs: pair_cost(inputs[0], inputs[1][:, :3]),
        (in_groups(src_sorted), in_groups(pair_cells)),
    )
    tgt_now = jnp.broadcast_to(tgt_own[:, None], (clusters, points))
    src_now = jnp.zeros((clusters, points), jnp.float32)
    for sweep in range(F_ITERS):
        sent_pot = tgt_now[asked_index].reshape(row_count, capacity, points)
        got_pot = lax.all_to_all(sent_pot, "rows", split_axis=0, concat_axis=0, tiled=True)
        pot_table = jnp.concatenate([tgt_now, got_pot.reshape(slot_total, points)], 0)
        pair_pot = pot_table[pair_index]

        def rows_of(inputs):
            cost_group, mass_group, pot_group, usable_now = inputs
            return fine_rows(cost_group, mass_group, pot_group, usable_now)

        src_now = lax.map(
            rows_of, (fcost, in_groups(pair_mass), in_groups(pair_pot), in_groups(usable))
        ).reshape(clusters, points)

        def parts_of(inputs):
            cost_group, mass_group, pot_group, usable_now = inputs
            return fine_parts(cost_group, mass_group, pot_group, usable_now)

        highs, sums = lax.map(
            parts_of, (fcost, in_groups(source_logmass), in_groups(src_now), in_groups(usable))
        )
        highs = highs.reshape(clusters, listed_slots, points)
        sums = sums.reshape(clusters, listed_slots, points)
        back_high = (
            jnp.full((slot_total, points), NEGATIVE, jnp.float32)
            .at[slot_of]
            .set(highs[:, 1:].reshape(-1, points), mode="drop")
        )
        back_sum = (
            jnp.zeros((slot_total, points), jnp.float32)
            .at[slot_of]
            .set(sums[:, 1:].reshape(-1, points), mode="drop")
        )
        got_high, got_sum = (
            lax.all_to_all(
                back_high.reshape(row_count, capacity, points),
                "rows",
                split_axis=0,
                concat_axis=0,
                tiled=True,
            ),
            lax.all_to_all(
                back_sum.reshape(row_count, capacity, points),
                "rows",
                split_axis=0,
                concat_axis=0,
                tiled=True,
            ),
        )
        got_high = got_high.reshape(slot_total, points)
        got_sum = got_sum.reshape(slot_total, points)
        best = jnp.maximum(
            highs[:, 0],
            jnp.max(jnp.where(matches[:, :, None], got_high[None, :, :], NEGATIVE), axis=1),
        )
        scaled = got_sum * jnp.exp(got_high - best[asked_index])
        combined = sums[:, 0] * jnp.exp(highs[:, 0] - best) + jnp.dot(
            match_table, scaled, precision=lax.Precision.HIGHEST
        )
        tgt_now = -TAU_F * EPS_F * (best + jnp.log(combined))
    return (src_now, tgt_now)


FEATURES = 32
CENTRE = 1.5
GROUP = 96
REST = 32
FIRST = 64
LOG2E = math.log2(math.e)
LN2 = math.log(2.0)


def three_parts(value):
    first = value.astype(jnp.bfloat16).astype(jnp.float32)
    left = value - first
    second = left.astype(jnp.bfloat16).astype(jnp.float32)
    return first, second, left - second


def coarse_start(stats):
    by_src = jnp.transpose(stats)
    cost = (by_src[:, 0:1] - stats[4:5]) ** 2
    cost = cost + (by_src[:, 1:2] - stats[5:6]) ** 2
    cost = (cost + (by_src[:, 2:3] - stats[6:7]) ** 2) / EPS_C
    return stats[7:8] - cost, by_src[:, 3:4] - cost


def coarse_sweep(to_src, to_tgt, tgt):
    scores = to_src + tgt / EPS_C
    highest = jnp.max(scores, axis=1, keepdims=True)
    summed = jnp.sum(jnp.exp(scores - highest), axis=1, keepdims=True)
    src = -TAU_C * EPS_C * (highest + jnp.log(summed))
    scores = to_tgt + src / EPS_C
    highest = jnp.max(scores, axis=0, keepdims=True)
    summed = jnp.sum(jnp.exp(scores - highest), axis=0, keepdims=True)
    return -TAU_C * EPS_C * (highest + jnp.log(summed))


def pack_kernel(src_coords, tgt_coords, src_logmass, tgt_logmass, listed, counts, out, blocks):
    own, points = src_logmass.shape
    slots = listed.shape[1]
    row = lax.axis_index("rows")
    col_count = lax.axis_size("cols")
    for axis in range(3):
        blocks[:, axis, :] = src_coords[axis]
        blocks[:, 4 + axis, :] = tgt_coords[axis]
    blocks[:, 3, :] = src_logmass[...]
    blocks[:, 7, :] = tgt_logmass[...]
    row_id = lax.broadcasted_iota(jnp.int32, (8, points), 0)
    lane = lax.broadcasted_iota(jnp.int32, (8, points), 1)
    known = jnp.zeros((8, points), jnp.float32)
    for q in range(own):
        block = blocks[q]
        highest = jnp.max(block, axis=1, keepdims=True)
        mass = highest + jnp.log(jnp.sum(jnp.exp(block - highest), axis=1, keepdims=True))
        mean = jnp.sum(block, axis=1, keepdims=True) / points
        value = jnp.where(row_id % 4 == 3, mass, mean)
        known = jnp.where(lane == row * own + q, value, known)
    pairs = own * slots
    for q in range(own):
        for k in range(slots):
            target = listed[q, k]
            place = target // (own * col_count) * own + target % own
            is_used = k < counts[q]
            at = pairs + q * slots + k
            known = jnp.where((row_id == row) & (lane == at), jnp.where(is_used, place, 0).astype(jnp.float32), known)
            known = jnp.where((row_id == row) & (lane == at + pairs), jnp.where(is_used, 1.0, 0.0), known)
    for q in range(own):
        out[q] = blocks[q]
    out[own] = known


def spread(bias, left, parts_ref):
    clusters, points = bias.shape
    for part, value in enumerate(three_parts(bias * LOG2E)):
        parts_ref[:, part, :] = value
    by_point = jnp.transpose(parts_ref[...].reshape(4 * clusters, points))
    for c in range(0, clusters, 2):
        shift = (FEATURES - 8 - 4 * c) % (4 * clusters)
        moved = (pltpu.roll(by_point, shift, 1) if shift else by_point).astype(jnp.bfloat16)
        left[c, :, FEATURES - 8 : FEATURES - 4] = moved[:, FEATURES - 8 : FEATURES - 4]
        left[c + 1, :, FEATURES - 4 : FEATURES] = moved[:, FEATURES - 4 : FEATURES]


def ready_kernel(
    near, far, known_ref, src_right, tgt_right, src_left, tgt_left, src_rows, tgt_rows, owner, owner_row_ref, lists_ref, parts_ref,
):
    clusters, points = src_rows.shape[1:]
    devices = known_ref.shape[0]
    own = clusters // devices
    half = devices // 2
    pairs = owner.shape[0]
    slots = pairs // clusters
    local_pairs = own * slots
    row_id = lax.broadcasted_iota(jnp.int32, (8, points), 0)
    lane_id = lax.broadcasted_iota(jnp.int32, (8, points), 1)
    row = lax.axis_index("rows")
    known = known_ref[...]

    for away in range(devices):
        held = near if away < half else far
        at = away % half * (own + 1)
        rows = pl.ds(lax.bitwise_xor(row, away) * own, own)
        for into, base in ((src_rows, 0), (tgt_rows, 4)):
            into[0, rows, :] = held[at : at + own, base + 3, :]
            square = jnp.zeros((own, points), jnp.float32)
            for axis in range(3):
                square = square + (held[at : at + own, base + axis, :] - CENTRE) ** 2
            into[1, rows, :] = square / EPS_F
    by_lane = jnp.transpose(known)
    first_pair = lax.broadcasted_iota(jnp.int32, (1, points), 1)
    owner_row = [jnp.zeros((1, points), jnp.float32) for _ in range(pairs // points)]
    used = []
    per_row = points // local_pairs
    for d in range(devices):
        held = by_lane[local_pairs : 2 * local_pairs, d : d + 1]
        owner[pl.ds(d * local_pairs, local_pairs), :] = jnp.broadcast_to(held, (local_pairs, points))
        used.append(jnp.broadcast_to(by_lane[2 * local_pairs : 3 * local_pairs, d : d + 1], (local_pairs, points)))
        shift = (d % per_row * local_pairs - local_pairs) % points
        moved = pltpu.roll(known, shift, 1) if shift else known
        start = d % per_row * local_pairs
        inside = (first_pair >= start) & (first_pair < start + local_pairs)
        owner_row[d // per_row] = jnp.where(inside, moved[d : d + 1], owner_row[d // per_row])
    used = jnp.concatenate(used, 0)
    target = owner[...]
    low = (row * own).astype(jnp.float32)
    mine = jnp.where((target >= low) & (target < low + own), used, 0.0)
    of_source = jnp.max(mine.reshape(clusters, slots, points), axis=1, keepdims=True)
    needed = used * jnp.broadcast_to(of_source, (clusters, slots, points)).reshape(pairs, points)
    before = lax.broadcasted_iota(jnp.int32, (pairs, pairs), 1) <= lax.broadcasted_iota(jnp.int32, (pairs, pairs), 0)
    before = jnp.where(before, 1.0, 0.0).astype(jnp.bfloat16)
    known_of = jnp.concatenate(owner_row, 1)
    owner_row_ref[...] = known_of
    pair_id = lax.broadcasted_iota(jnp.int32, (8, pairs), 1).astype(jnp.float32)
    odd_row = lax.broadcasted_iota(jnp.int32, (8, pairs), 0) % 2 == 1
    pair_id = jnp.where(odd_row, known_of, pair_id).astype(jnp.bfloat16)
    place_id = lax.broadcasted_iota(jnp.int32, (pairs, points), 1).astype(jnp.float32) + 1.0
    lists_ref[...] = jnp.zeros(lists_ref.shape, jnp.int32)
    for which, mask in enumerate((used, needed, mine)):
        place = jnp.dot(before, mask.astype(jnp.bfloat16), preferred_element_type=jnp.float32)
        for part in range(pairs // points):
            hit = jnp.where(place == place_id + float(part * points), mask, 0.0).astype(jnp.bfloat16)
            order = jnp.dot(pair_id, hit, preferred_element_type=jnp.float32)
            lists_ref[2 * which : 2 * which + 2, pl.ds(part * points, points)] = order[:2].astype(jnp.int32)
        lists_ref[2 * which : 2 * which + 2, pl.ds(pairs, points)] = jnp.where(
            lane_id[:2] == points - 1, jnp.broadcast_to(place[pairs - 1 :], (2, points)), 0.0
        ).astype(jnp.int32)

    picked = jnp.where(row_id % 4 < 3, 1.0, 0.0)
    none = jnp.zeros((8, points), jnp.float32)

    def prepare(c, coords, order, right, left):
        parts = three_parts(coords)
        groups = [parts[one] + jnp.roll(parts[two], 3, 0) for one, two in order]
        right[c] = jnp.concatenate(groups + [picked], 0).astype(jnp.bfloat16)
        left[c] = jnp.transpose(jnp.concatenate(groups + [none], 0)).astype(jnp.bfloat16)

    def some(at, carry):
        for held, first in ((near, 0), (far, half)):
            for q in range(own):
                block = held[at * (own + 1) + q]
                c = lax.bitwise_xor(row, at + first) * own + q
                coords = jnp.where(row_id < 3, block - CENTRE, 0.0)
                prepare(c, coords, ((0, 0), (1, 1), (0, 2)), src_right, src_left)
                coords = jnp.where(row_id < 3, (jnp.roll(block, -4, 0) - CENTRE) * (2.0 / EPS_F * LOG2E), 0.0)
                prepare(c, coords, ((0, 1), (0, 1), (2, 0)), tgt_right, tgt_left)
        return carry

    lax.fori_loop(0, half, some, 0)
    parts_ref[...] = jnp.zeros((clusters, 4, points), jnp.float32)
    spread(tgt_rows[0] - tgt_rows[1], tgt_left, parts_ref)


def fine_kernel(
    known, second, third, fourth, src_right, tgt_right, src_rows, tgt_rows, owner, owner_row, lists_ref, src_left_in, tgt_left_in,
    src_out, tgt_out, src_left, tgt_left,
    parts_ref, highs, sums, src_pot, best_rows, to_src, to_tgt, lists, copied,
):
    move = pltpu.make_async_copy(lists_ref, lists, copied)
    move.start()
    clusters, points = src_pot.shape
    own = src_out.shape[0]
    pairs = highs.shape[0]
    slots = pairs // clusters
    lane_id = lax.broadcasted_iota(jnp.int32, (8, points), 1)
    row = lax.axis_index("rows")

    def pair_pass(which, by_target, beside=None):
        left, right = (src_left, tgt_right) if by_target else (tgt_left, src_right)

        count = lists[2 * which, pairs + points - 1]

        def some(start, size):
            for lane in range(size):
                pair = lists[2 * which, start + lane]
                src = lax.shift_right_logical(pair, slots.bit_length() - 1)
                tgt = lists[2 * which + 1, start + lane]
                row, col = (src, tgt) if by_target else (tgt, src)
                scores = jnp.dot(left[row], right[col], preferred_element_type=jnp.float32)
                highest = jnp.max(scores, axis=0, keepdims=True)
                highs[pl.ds(pair, 1), :] = highest
                sums[pl.ds(pair, 1), :] = jnp.sum(jnp.exp2(scores - highest), axis=0, keepdims=True)

        state, done = None, 0
        if beside is not None:

            def both(at, state):
                some(at * FIRST, FIRST)
                return beside(beside(state))

            state = lax.fori_loop(0, C_ITERS // 2, both, jnp.zeros((1, points), jnp.float32))
            done = C_ITERS // 2 * FIRST

        def many(at, carry):
            some(done + at * GROUP, GROUP)
            return carry

        def few(at, carry):
            some(at * REST, REST)
            return carry

        if which < 2:
            steps = jnp.maximum(lax.div(count - done, GROUP), 0)
            lax.fori_loop(0, steps, many, 0)
            done = done + steps * GROUP

        lax.fori_loop(lax.div(done, REST), lax.div(count + (REST - 1), REST), few, 0)
        return state

    def by_pair(rows):
        lane = lax.broadcasted_iota(jnp.int32, (pairs, points), 1)
        picks = jnp.where((lane >= FEATURES) & ((lane % clusters).astype(jnp.float32) == owner[...]), 1.0, 0.0)
        parts = jnp.concatenate((jnp.zeros((FEATURES, points), jnp.float32),) + three_parts(rows), 0)
        return jnp.dot(picks.astype(jnp.bfloat16), parts.astype(jnp.bfloat16), preferred_element_type=jnp.float32)

    def src_update(high):
        high = high.reshape(clusters, slots, points)
        best = jnp.max(high, axis=1)
        total = jnp.sum(sums[...].reshape(clusters, slots, points) * jnp.exp2(high - best[:, None, :]), axis=1)
        value = -TAU_F * EPS_F * (LN2 * (best + jnp.log2(total)) - src_rows[1])
        src_pot[...] = value
        return src_rows[0] + value / EPS_F - src_rows[1]

    def best_of(t):
        return jnp.max(jnp.where(owner[...] == t.astype(jnp.float32), highs[...], NEGATIVE), axis=0, keepdims=True)

    def tgt_merge():
        width = math.gcd(clusters, 4)

        def find(at, carry):
            for step in range(width):
                best_rows[pl.ds(at * width + step, 1), :] = best_of(at * width + step)
            return carry

        lax.fori_loop(0, clusters // width, find, 0)
        best = best_rows[...]
        weighted = three_parts(sums[...] * jnp.exp2(highs[...] - by_pair(best)))
        number = lax.broadcasted_iota(jnp.int32, (clusters, pairs), 0)
        gather = jnp.where(number.astype(jnp.float32) == owner_row[...], 1.0, 0.0).astype(jnp.bfloat16)
        total = sum(
            jnp.dot(gather, part.astype(jnp.bfloat16), preferred_element_type=jnp.float32) for part in weighted
        )
        return LN2 * (best + jnp.log2(total))

    parts_ref[...] = jnp.zeros((clusters, 4, points), jnp.float32)
    highs[...] = jnp.full((pairs, points), NEGATIVE, jnp.float32)
    sums[...] = jnp.zeros((pairs, points), jnp.float32)
    stats = jnp.where(lane_id < clusters, known[...], 0.0)
    for away, other in enumerate((second, third, fourth), 1):
        inside = (lane_id >= away * clusters) & (lane_id < (away + 1) * clusters)
        stats = jnp.where(inside, pltpu.roll(other[...], away * clusters, 1), stats)
    to_src[...], to_tgt[...] = coarse_start(stats)
    move.wait()
    first_own = row * own
    coarse = pair_pass(0, False, lambda tgt: coarse_sweep(to_src[...], to_tgt[...], tgt))
    coarse = jnp.transpose(jnp.broadcast_to(coarse, (points, points)))[:clusters]
    spread(src_update(highs[...] + by_pair(coarse * (LOG2E / EPS_F))), src_left, parts_ref)
    for sweep in range(1, F_ITERS):
        pair_pass(0, True)
        value = -TAU_F * EPS_F * (tgt_merge() - tgt_rows[1])
        spread(tgt_rows[0] + value / EPS_F - tgt_rows[1], tgt_left, parts_ref)
        pair_pass(1 if sweep == F_ITERS - 1 else 0, False)
        spread(src_update(highs[...]), src_left, parts_ref)
    pair_pass(2, True)
    for c in range(own):
        t = first_own + c
        best = best_of(t)
        mine = jnp.where(owner[...] == t.astype(jnp.float32), sums[...] * jnp.exp2(highs[...] - best), 0.0)
        total = LN2 * (best + jnp.log2(jnp.sum(mine, axis=0, keepdims=True)))
        tgt_out[pl.ds(c, 1), :] = -TAU_F * EPS_F * (total - tgt_rows[1, pl.ds(t, 1), :])
        src_out[pl.ds(c, 1), :] = src_pot[pl.ds(t, 1), :]


def local_gathered(source_coords, target_coords, source_logmass, target_logmass, pair_targets, pair_counts):
    own, points = source_coords.shape[1:]
    slots = pair_targets.shape[1]
    row_count = lax.axis_size("rows")
    clusters = own * row_count
    pairs = clusters * slots
    whole = pl.BlockSpec(memory_space=pltpu.VMEM)
    scalars = pl.BlockSpec(memory_space=pltpu.SMEM)
    packed = pl.pallas_call(
        pack_kernel,
        out_shape=pltpu.VMEM((own + 1, 8, points), jnp.float32),
        in_specs=[whole] * 4 + [scalars] * 2,
        out_specs=whole,
        scratch_shapes=[pltpu.VMEM((own, 8, points), jnp.float32)],
        name="pack",
    )(source_coords, target_coords, source_logmass, target_logmass, pair_targets, pair_counts)

    def from_row(value, away):
        return lax.ppermute(value, "rows", [(r, r ^ away) for r in range(row_count)])

    near = jnp.concatenate([packed] + [from_row(packed, away) for away in range(1, 4)], 0)
    far = from_row(near, 4)
    held = jnp.stack([near, far]).reshape(row_count, own + 1, 8, points)
    known = [jnp.sum(held[:, own], axis=0)]
    for away in range(1, 4):
        known.append(lax.ppermute(known[0], "cols", [(c, c ^ away) for c in range(4)]))
    features = jax.ShapeDtypeStruct((clusters, FEATURES, points), jnp.bfloat16)
    by_point = jax.ShapeDtypeStruct((clusters, points, FEATURES), jnp.bfloat16)
    rows = jax.ShapeDtypeStruct((2, clusters, points), jnp.float32)
    ready = pl.pallas_call(
        ready_kernel,
        out_shape=(
            features,
            features,
            by_point,
            by_point,
            rows,
            rows,
            jax.ShapeDtypeStruct((pairs, points), jnp.float32),
            jax.ShapeDtypeStruct((1, pairs), jnp.float32),
            jax.ShapeDtypeStruct((8, pairs + points), jnp.int32),
        ),
        in_specs=[whole] * 3,
        out_specs=(whole,) * 9,
        scratch_shapes=[pltpu.VMEM((clusters, 4, points), jnp.float32)],
        compiler_params=pltpu.CompilerParams(vmem_limit_bytes=12 * 2**20),
        cost_estimate=pl.CostEstimate(flops=4 * 10**6, bytes_accessed=4 * 10**6, transcendentals=0),
        name="ready",
    )(near, far, known[0])
    src_right, tgt_right, src_left, tgt_left, src_rows, tgt_rows, owner, owner_row, lists = ready
    source, target, _, _ = pl.pallas_call(
        fine_kernel,
        out_shape=(jax.ShapeDtypeStruct((own, points), jnp.float32),) * 2 + (by_point,) * 2,
        in_specs=[whole] * 13,
        out_specs=(whole,) * 4,
        input_output_aliases={11: 2, 12: 3},
        scratch_shapes=[
            pltpu.VMEM((clusters, 4, points), jnp.float32),
            pltpu.VMEM((pairs, points), jnp.float32),
            pltpu.VMEM((pairs, points), jnp.float32),
            pltpu.VMEM((clusters, points), jnp.float32),
            pltpu.VMEM((clusters, points), jnp.float32),
            pltpu.VMEM((points, points), jnp.float32),
            pltpu.VMEM((points, points), jnp.float32),
            pltpu.SMEM((8, pairs + points), jnp.int32),
            pltpu.SemaphoreType.DMA(()),
        ],
        compiler_params=pltpu.CompilerParams(
            vmem_limit_bytes=12 * 2**20
        ),
        name="fine",
    )(*known, src_right, tgt_right, src_rows, tgt_rows, owner, owner_row, lists, src_left, tgt_left)
    return source, target


def solution(mesh):
    columns = mesh.shape["rows"]

    def local(*args):
        clusters, points = args[0].shape[1:]
        slots = args[4].shape[1]
        fits = clusters * columns * 4 == points and 3 * clusters * slots <= points and slots * columns * clusters % points == 0
        if mesh.shape["cols"] == 4 and columns == slots == 8 and clusters * slots == 32 and fits:
            return local_gathered(*args)
        return local_exchanged(*args)

    return jax.shard_map(
        local,
        mesh=mesh,
        in_specs=(
            P(None, ("rows", "cols"), None),
            P(None, ("rows", "cols"), None),
            P(("rows", "cols"), None),
            P(("rows", "cols"), None),
            P(("rows", "cols"), None),
            P(("rows", "cols")),
        ),
        out_specs=(P(("rows", "cols"), None), P(("rows", "cols"), None)),
        check_vma=False,
    )
```
